32 devices in a mesh: pp: 4 (over z), ep: 8 (over y, x, core).
Axes of the slice: x: 2, y: 2, z: 4, core: 2. Of those that a mesh axis runs over, the one named last changes fastest.
Arguments:
- inputs: bfloat16 [4, 128, 7168], P(None, 'ep'), may hold values from -16 to 16
- norm_gain: float32 [4, 7168], P('pp'), may hold values from 0.25 to 1.75
- router_weight: bfloat16 [4, 7168, 4], P('pp'), may hold values from -0.0625 to 0.0625
- gate_weight: bfloat16 [4, 7168, 4096], P('pp', None, 'ep'), may hold values from -0.0625 to 0.0625
- up_weight: bfloat16 [4, 7168, 4096], P('pp', None, 'ep'), may hold values from -0.0625 to 0.0625
- down_weight: bfloat16 [4, 1024, 28672], P('pp', None, 'ep'), may hold values from -0.1875 to 0.1875
- routing: int32 [4, 4, 128, 2], P('pp', None, 'ep'), may hold values from 0 to 3, all different within a row; in each aligned block of 16 rows (0 to 15, 16 to 31, ..., all dimensions but the last counted through in order) at most 10 rows name the same one
Outputs:
- final: bfloat16 [4, 128, 7168], P('pp', 'ep')
The draws below stay inside these ranges and needn't reach their ends.
Inputs may be any that keep to these rules, and one draw needn't show every extreme that they name: `routing`: each token names 2 different experts. Among the 16 tokens of one device in one micro-batch of one layer, no expert is named more than 10 times, and in some of these aligned blocks one expert is named exactly 10 times.
All inputs are finite; a program needn't handle non-finite values.
Results may differ from the reference program's by a relative error of at most 0.025.
Values may be sent and summed in bfloat16 or wider, within the bound.
A program may use at most 128 MiB of HBM per device.

```python
import math
import jax
import jax.numpy as jnp
import numpy as np
from jax import lax

D = 7168
HID = 1024
TOPK = 2
TOK_DEV = 16
EXPERTS = 4
MOST = 10
MB = 4
LAYERS = 4
TOKENS = 128
N_EP = 8


def draw_inputs(key, part):
    key_rows = jax.random.fold_in(key, 11)
    key_values = jax.random.fold_in(key, 12)
    values = jnp.clip(jax.random.normal(key_values, (MB, TOKENS, D), jnp.float32), -4.0, 4.0)
    row_scale = jnp.exp(jax.random.uniform(key_rows, (MB, TOKENS, 1), jnp.float32, math.log(0.4), math.log(4.0)))
    return (values * row_scale).astype(jnp.bfloat16)


def level_of(rng, extent, cuts, least, high):
    level, own = 1.0, jax.random.fold_in(rng, 6)
    for position, blocks in cuts:
        draws = jnp.exp(jax.random.uniform(jax.random.fold_in(own, position), (blocks,), jnp.float32, least / len(cuts), high / len(cuts)))
        level = level * jnp.repeat(draws, extent[position] // blocks).reshape([-1 if axis == position else 1 for axis in range(len(extent))])
    return level


def shared_out(own_key, own, number, rows, number_of, top, reach, lean):
    ranking = jax.random.permutation(own_key, number_of)
    heavy_load, usual = load_shares(number_of, rows * top, reach, lean, True), load_shares(number_of, rows * top, reach, lean, False)
    places = jnp.arange(number_of)

    def named(lengths, rotation):
        used = int((lengths > 0).sum())
        fixed = max(1, used // 4)
        passed = fixed + (places - fixed + rotation * (used - fixed)) % max(1, number_of - fixed)
        return jnp.zeros((number_of,), jnp.int32).at[ranking[jnp.where(places < fixed, places, passed)]].set(jnp.asarray(lengths, jnp.int32))

    lengths = jnp.where(number % 4 == 0, named(heavy_load, number // 4), named(usual, number - number // 4 - 1))
    mixed = jax.random.permutation(jax.random.fold_in(own, 3), number_of)
    giver, sink = mixed[0:number_of // 2 * 2:2], mixed[1:number_of // 2 * 2:2]
    slack = jnp.minimum(lengths[giver] - 1, reach - lengths[sink]) // 2
    slack = jnp.where((giver == ranking[0]) | (sink == ranking[0]) | (lengths[sink] == 0), 0, jnp.maximum(slack, 0))
    passed = jax.random.randint(jax.random.fold_in(own, 4), (number_of // 2,), 0, 1 << 20) % (slack + 1)
    lengths = lengths.at[giver].add(-passed).at[sink].add(passed)
    labels = jnp.searchsorted(jnp.cumsum(lengths), jnp.arange(rows * top), side="right").astype(jnp.int32)
    listing = labels.reshape(top, rows).T
    listing = listing[jax.random.permutation(jax.random.fold_in(own, 1), rows)]
    rotation = jax.random.randint(jax.random.fold_in(own, 2), (rows, 1), 0, top)
    return jnp.take_along_axis(listing, (jnp.arange(top)[None, :] + rotation) % top, axis=1)


def load_shares(amount, total, bound, skew, full):
    loads = [(1 << 20) // math.isqrt(standing ** skew) + 1 for standing in range(1, amount + 1)]
    largest = bound if full else min(bound, max(-(-total // amount), total * loads[0] // sum(loads)))
    least = 1 if total - largest >= amount - 1 else 0
    given, spare = [largest] + [least] * (amount - 1), total - largest - least * (amount - 1)
    while spare > 0:
        free = [i for i in range(1, amount) if given[i] < largest] or [i for i in range(1, amount) if given[i] < bound]
        pool, remaining = sum([loads[i] for i in free]), spare
        for i in free:
            more = min(bound - given[i], max(1, remaining * loads[i] // pool), spare)
            given[i] = given[i] + more
            spare = spare - more
    return np.array(given)


def bell_draw(own_key, dims, scale, bound, cuts=(), kind=jnp.bfloat16):
    result = jax.random.normal(own_key, dims, jnp.float32) * scale
    if len(cuts) > 0:
        result = level_of(own_key, dims, cuts, -0.22, 0.18) * result
    return jnp.clip(result, min=-bound, max=bound).astype(kind)


def setup_inputs(seed: int = 0) -> dict:
    splits = jax.random.split(jax.random.key(seed), 8)
    inputs = draw_inputs(jax.random.fold_in(splits[7], 71), 0)
    norm_gain = jnp.clip(1.0 + 0.15 * jax.random.normal(splits[1], (LAYERS, D), jnp.float32), 0.25, 1.75)
    router_weight = bell_draw(splits[2], (LAYERS, D, EXPERTS), D ** -0.5, 0.0625, ((0, 4),))
    gate_weight = bell_draw(splits[3], (LAYERS, D, EXPERTS * HID), D ** -0.5, 0.0625, ((0, 4), (2, 8)))
    up_weight = bell_draw(splits[4], (LAYERS, D, EXPERTS * HID), D ** -0.5, 0.0625, ((0, 4), (2, 8)))
    down_weight = bell_draw(splits[5], (LAYERS, HID, EXPERTS * D), HID ** -0.5, 0.1875, ((0, 4), (2, 8)))
    routing_keys = jax.random.split(jax.random.fold_in(splits[6], 1), LAYERS * MB * TOKENS // TOK_DEV)
    routing_turns = jax.random.permutation(jax.random.fold_in(splits[6], 3), LAYERS * MB * TOKENS // TOK_DEV)
    routing = jax.vmap(lambda own, number: shared_out(jax.random.fold_in(splits[6], 2), own, number, TOK_DEV, EXPERTS, TOPK, MOST, 2))(routing_keys, routing_turns).reshape((LAYERS, MB, TOKENS, TOPK))
    return {"inputs": inputs, "norm_gain": norm_gain, "router_weight": router_weight, "gate_weight": gate_weight, "up_weight": up_weight, "down_weight": down_weight, "routing": routing}


routed_scale = 2.5
norm_epsilon = 1e-06

def expert_rows(rows, gate_block, up_block, down_block):
    gate_proj = jnp.dot(rows, gate_block, preferred_element_type=jnp.float32)
    up_proj = jnp.dot(rows, up_block, preferred_element_type=jnp.float32)
    hidden = (jax.nn.silu(gate_proj) * up_proj).astype(jnp.bfloat16)
    return jnp.dot(hidden, down_block, preferred_element_type=jnp.float32).astype(jnp.bfloat16)

def moe_layer(activations, gain_row, router, gate_all, up_all, down_all, routes):
    current = activations.astype(jnp.float32)
    mean_square = lax.optimization_barrier(jnp.mean(current * current, axis=1, keepdims=True))
    normed = (current * lax.rsqrt(mean_square + norm_epsilon) * gain_row).astype(jnp.bfloat16)
    scores = jax.nn.sigmoid(jnp.dot(normed, router, preferred_element_type=jnp.float32))
    expert_ids = jnp.arange(EXPERTS, dtype=jnp.int32)
    onehot = (routes[:, :, None] == expert_ids[None, None, :]).astype(jnp.float32)
    picked = lax.optimization_barrier(jnp.sum(onehot * scores[:, None, :], axis=2))
    mixing = routed_scale * picked / lax.optimization_barrier(jnp.sum(picked, axis=1, keepdims=True))
    expert_mix = lax.optimization_barrier(jnp.sum(onehot * mixing[:, :, None], axis=1))
    chosen = lax.optimization_barrier(jnp.sum(onehot, axis=1)) > 0.5
    capacity = N_EP * MOST

    def one_expert(expert):
        column = chosen[:, expert]
        members = jnp.nonzero(column, size=capacity, fill_value=0)[0].astype(jnp.int32)
        live_count = jnp.sum(column.astype(jnp.int32))
        is_live = jnp.arange(capacity, dtype=jnp.int32) < live_count
        gate_block = lax.dynamic_slice_in_dim(gate_all, expert * HID, HID, 1)
        up_block = lax.dynamic_slice_in_dim(up_all, expert * HID, HID, 1)
        down_block = lax.dynamic_slice_in_dim(down_all, expert * D, D, 1)
        outcome = expert_rows(normed[members], gate_block, up_block, down_block)
        share_weight = jnp.where(is_live, expert_mix[members, expert], 0.0)
        return (members, share_weight[:, None] * outcome.astype(jnp.float32))
    members, contributions = lax.map(one_expert, expert_ids)
    combined = jnp.zeros((TOKENS, D), jnp.float32).at[members.reshape(-1)].add(contributions.reshape(-1, D))
    return (current + combined).astype(jnp.bfloat16)

def reference(inputs, norm_gain, router_weight, gate_weight, up_weight, down_weight, routing):

    def one_batch(batch_index):

        def one_layer(activations, layer_index):
            updated = moe_layer(activations, norm_gain[layer_index], router_weight[layer_index], gate_weight[layer_index], up_weight[layer_index], down_weight[layer_index], routing[layer_index, batch_index])
            return (updated, None)
        finished, unused = lax.scan(one_layer, inputs[batch_index], jnp.arange(LAYERS, dtype=jnp.int32))
        return finished
    return lax.map(one_batch, jnp.arange(MB, dtype=jnp.int32))
```

```python
import functools

import jax
import jax.numpy as jnp
from jax import lax
from jax.experimental import pallas as pl
from jax.experimental.pallas import tpu as pltpu
from jax.sharding import PartitionSpec as P

routed_scale = 2.5
norm_epsilon = 1e-06
lane = 128
tile_rows = 16
f32, bf16 = jnp.float32, jnp.bfloat16


class Plan:
    def __init__(self, n_pp, n_ep, micros, rows, width, experts, top, hid):
        self.n_pp, self.n_ep, self.n_pair = n_pp, n_ep, n_ep // 2
        self.micros, self.rows, self.width = micros, rows, width
        self.experts, self.top, self.hid = experts, top, hid
        self.half = width // 2
        self.pair_rows = 2 * rows
        most = rows * top * 5 // (4 * experts)
        slots = 2 * most
        main = tile_rows * max(1, slots // tile_rows)
        extra = max(0, slots - main)
        if extra > tile_rows // 2:
            main, extra = main + tile_rows, 0
        self.main = main
        self.rem = 0 if extra == 0 else (4 if extra <= 4 else 8)
        self.tiles = tile_rows // self.rem if self.rem else 4
        self.unit = lane * self.tiles
        self.pack = self.unit + (lane if self.rem else 0)
        self.units = self.half // self.unit
        self.main_rows = self.n_pair * self.main
        self.rem_rows = self.n_pair * self.rem
        self.work_rows = self.main_rows + self.rem_rows
        self.lanes_main = experts * self.main
        self.lanes_rem = experts * tile_rows
        count = min(3, self.units)
        cuts = [self.units * g // count for g in range(count + 1)]
        self.groups = list(zip(cuts[:-1], cuts[1:]))


def kernel(
    plan,
    inputs_hbm, gain_ref, router_ref, gate_hbm, up_hbm, down_hbm, routing_ref,
    out_ref,
    routes, xs, fin, dsend, drecv, dpart, csend, crecv, wg, wu, wd,
    lhs, ssq, acc_g, acc_u, acc_d, hid_own, hid_par, stat_own, stat_par,
    pick_main, pick_rem, place_main, place_rem, targets,
    weight_sem, init_sem, route_send, route_recv, init_send, init_recv,
    disp_send, disp_recv, fwd_send, fwd_recv, hid_send, hid_recv,
    comb_send, comb_recv, stat_send, stat_recv, relay_send, relay_recv, fin_send, fin_recv,
):
    section = lax.axis_index("pp")
    me = lax.axis_index("ep")
    core, pair = me % 2, me // 2
    last = plan.n_pp - 1
    n_pair, rows, half, unit, pack = plan.n_pair, plan.rows, plan.half, plan.unit, plan.pack
    pair_rows, experts, top = plan.pair_rows, plan.experts, plan.top
    groups = plan.groups
    micros = plan.micros
    own_half = pl.multiple_of(core * half, lane)
    par_half = pl.multiple_of((1 - core) * half, lane)
    own_block = pl.multiple_of(core * rows, rows)
    partner = {"ep": me + 1 - 2 * core}

    def flip(value, mask):
        for b in range((n_pair - 1).bit_length()):
            if mask >> b & 1:
                value = value + (1 << b) - 2 * (1 << b) * ((value // (1 << b)) % 2)
        return value

    def remote(src, dst, send, recv, where):
        return pltpu.make_async_remote_copy(
            src_ref=src, dst_ref=dst, send_sem=send, recv_sem=recv,
            device_id=where, device_id_type=pl.DeviceIdType.MESH,
        )

    def dot(a, b):
        return jnp.dot(a, b, preferred_element_type=f32)

    weight_copies = [
        pltpu.make_async_copy(gate_hbm.at[0], wg, weight_sem.at[0]),
        pltpu.make_async_copy(up_hbm.at[0], wu, weight_sem.at[1]),
        pltpu.make_async_copy(down_hbm.at[0], wd, weight_sem.at[2]),
    ]

    def init_local(micro):
        return pltpu.make_async_copy(
            inputs_hbm.at[micro, :, pl.ds(own_half, half)],
            xs.at[micro, pl.ds(own_block, rows), :], init_sem.at[micro],
        )

    def init_copy(micro):
        return remote(
            inputs_hbm.at[micro, :, pl.ds(par_half, half)],
            xs.at[micro, pl.ds(own_block, rows), :],
            init_send.at[micro], init_recv.at[micro], partner,
        )

    route_copy = remote(routing_ref, routes.at[core], route_send, route_recv, partner)

    def cols(group):
        return pl.ds(group[0] * unit, (group[1] - group[0]) * unit)

    def pack_cols(group):
        return pl.ds(group[0] * pack, (group[1] - group[0]) * pack)

    def disp_copy(micro, g, rel):
        to = flip(pair, rel)
        return remote(
            dsend.at[micro % 2, to, :, pack_cols(groups[g])],
            drecv.at[micro, pair, :, pack_cols(groups[g])],
            disp_send.at[micro % 2, g, rel], disp_recv.at[micro, g, rel],
            {"ep": 2 * to + core},
        )

    def fwd_copy(micro, g):
        return remote(
            drecv.at[micro, :, :, pack_cols(groups[g])],
            dpart.at[micro, :, :, pack_cols(groups[g])],
            fwd_send.at[micro, g], fwd_recv.at[micro, g], partner,
        )

    def hid_copy(micro):
        return remote(
            hid_own.at[micro % 2], hid_par.at[micro], hid_send.at[micro % 2], hid_recv.at[micro],
            partner,
        )

    def comb_copy(micro, g, rel):
        to = flip(pair, rel)
        return remote(
            csend.at[micro % 2, to, :, pack_cols(groups[g])],
            crecv.at[micro, pair, :, pack_cols(groups[g])],
            comb_send.at[micro % 2, g, rel], comb_recv.at[micro, g, rel],
            {"ep": 2 * to + core},
        )

    def stat_copy(micro):
        return remote(
            stat_own.at[micro], stat_par.at[micro], stat_send.at[micro], stat_recv.at[micro], partner
        )

    def relay_copy(micro, g):
        ref = xs.at[micro, :, cols(groups[g])]
        return remote(
            ref, ref, relay_send.at[micro, g], relay_recv.at[micro, g],
            {"pp": (section + 1) % plan.n_pp},
        )

    def fin_cols(half_start, g):
        start = pl.multiple_of(half_start + groups[g][0] * unit, lane)
        return pl.ds(start, (groups[g][1] - groups[g][0]) * unit)

    def final_copy(micro, g, block):
        return remote(
            xs.at[micro, pl.ds(block * rows, rows), cols(groups[g])],
            fin.at[:, fin_cols(own_half, g)],
            fin_send.at[micro, g, block], fin_recv.at[core, g],
            {"pp": micro, "ep": 2 * pair + block},
        )

    def final_partner_copy(g):
        return remote(
            xs.at[micros - 1, pl.ds(pl.multiple_of((1 - core) * rows, rows), rows), cols(groups[g])],
            fin.at[:, fin_cols(own_half, g)],
            fin_send.at[micros - 1, g, 0], fin_recv.at[core, g], partner,
        )

    @pl.when(section == 0)
    def _():
        for micro in range(micros):
            init_local(micro).start()

    for copy in weight_copies:
        copy.start()

    barrier = pltpu.get_barrier_semaphore()
    greeted = [{"ep": 2 * flip(pair, rel) + core} for rel in range(1, n_pair)] + [partner]
    for step in range(1, plan.n_pp):
        other = (section + step) % plan.n_pp
        greeted += [{"pp": other}, {"pp": other, "ep": me + 1 - 2 * core}]
    for device in greeted:
        pl.semaphore_signal(barrier, inc=1, device_id=device, device_id_type=pl.DeviceIdType.MESH)
    pl.semaphore_wait(barrier, len(greeted))

    route_copy.start()

    @pl.when(section == 0)
    def _():
        for micro in range(micros):
            init_copy(micro).start()

    routes[core] = routing_ref[...]
    route_copy.wait()

    def make_selections(micro, unused):
        names = jnp.concatenate([routes[0, micro], routes[1, micro]], axis=1)
        expert = lax.broadcasted_iota(jnp.int32, (experts, pair_rows), 0)
        hit = [expert == names[k : k + 1] for k in range(top)]
        chosen = functools.reduce(jnp.logical_or, hit)
        before = lax.broadcasted_iota(jnp.int32, (pair_rows, pair_rows), 0)
        after = lax.broadcasted_iota(jnp.int32, (pair_rows, pair_rows), 1)
        rank = dot(
            jnp.where(chosen, 1.0, 0.0).astype(bf16),
            jnp.where(before < after, 1.0, 0.0).astype(bf16),
        )
        main_target, rem_target, columns = [], [], []
        lanes = lax.broadcasted_iota(jnp.int32, (pair_rows, lane), 1)
        kept = jnp.zeros((pair_rows, lane), jnp.int32)
        for k in range(top):
            slot = jnp.sum(jnp.where(hit[k], rank, 0.0), axis=0, keepdims=True).astype(jnp.int32)
            name = names[k : k + 1]
            main_target.append(jnp.where(slot < plan.main, name * plan.main + slot, -1))
            rem_target.append(
                jnp.where(slot >= plan.main, name * tile_rows + slot - plan.main, -tile_rows * experts)
            )

            def column(row):
                return jnp.sum(
                    jnp.where(before == after, row, 0).astype(f32), axis=1, keepdims=True
                ).astype(jnp.int32)

            columns.append((column(main_target[k]), column(rem_target[k])))
            kept = jnp.where(lanes == k, column(name), kept)
        targets[micro] = kept
        spot = lax.broadcasted_iota(jnp.int32, (plan.lanes_main, pair_rows), 0)
        picks = functools.reduce(jnp.logical_or, [spot == target for target in main_target])
        pick_main[micro] = jnp.where(picks, 1.0, 0.0).astype(bf16)
        spot = lax.broadcasted_iota(jnp.int32, (pair_rows, plan.lanes_main), 1)
        place_main[micro] = jnp.concatenate(
            [jnp.where(spot == columns[k][0], 1.0, 0.0) for k in range(top)], axis=0
        ).astype(bf16)
        if plan.rem:
            spot = lax.broadcasted_iota(jnp.int32, (plan.lanes_rem, pair_rows), 0)
            pick_rem[micro] = jnp.concatenate(
                [
                    jnp.where(
                        functools.reduce(
                            jnp.logical_or, [spot == target + t * plan.rem for target in rem_target]
                        ),
                        1.0, 0.0,
                    )
                    for t in range(plan.tiles)
                ],
                axis=1,
            ).astype(bf16)
            spot = lax.broadcasted_iota(jnp.int32, (pair_rows, plan.lanes_rem), 1)
            place_rem[micro] = jnp.concatenate(
                [
                    jnp.where(spot == columns[k][1] + t * plan.rem, 1.0, 0.0)
                    for t in range(plan.tiles)
                    for k in range(top)
                ],
                axis=0,
            ).astype(bf16)
        return unused

    lax.fori_loop(0, micros, make_selections, 0)

    if plan.rem:
        size = n_pair * tile_rows
        row = lax.broadcasted_iota(jnp.int32, (size, size), 0)
        column = lax.broadcasted_iota(jnp.int32, (size, size), 1)
        rem, tiles = plan.rem, plan.tiles

        def by_tile(index):
            tile, rest = index // (n_pair * rem), index % (n_pair * rem)
            return (rest // rem) * tile_rows + tile * rem + rest % rem

        to_rows = jnp.where(by_tile(row) == column, 1.0, 0.0).astype(bf16)
        to_tiles = jnp.where(by_tile(column) == row, 1.0, 0.0).astype(bf16)

    def dispatch(micro):
        @pl.when(micro >= 2)
        def _():
            for g in range(len(groups)):
                for rel in range(1, n_pair):
                    disp_copy(micro, g, rel).wait_send()

        @pl.when(section == 0)
        def _():
            init_local(micro).wait()
            init_copy(micro).wait()

        pick = pick_main[micro]
        for g, group in enumerate(groups):

            @pl.when(section > 0)
            def _():
                relay_copy(micro, g).wait_recv()

            for u in range(*group):
                x = xs[micro, :, pl.ds(u * unit, unit)]
                packed = dot(pick, x).astype(bf16)
                dsend[micro % 2, :, :, pl.ds(u * pack, unit)] = packed.reshape(
                    experts, plan.main, unit
                )
                if plan.rem:
                    stacked = jnp.concatenate(
                        [x[:, t * lane : (t + 1) * lane] for t in range(plan.tiles)], axis=0
                    )
                    packed = dot(pick_rem[micro], stacked).astype(bf16)
                    dsend[micro % 2, :, :, pl.ds(u * pack + unit, lane)] = packed.reshape(
                        experts, tile_rows, lane
                    )
            for rel in range(1, n_pair):
                disp_copy(micro, g, rel).start()
            drecv[micro, pair, :, pack_cols(group)] = dsend[micro % 2, pair, :, pack_cols(group)]

    def statistics(micro):
        x = xs[micro].astype(f32)
        lanes = lax.broadcasted_iota(jnp.int32, (pair_rows, lane), 1)
        stat = jnp.where(lanes == experts, jnp.sum(x * x, axis=1, keepdims=True), 0.0)
        scaled = x * gain_ref[:, pl.ds(own_half, half)]
        for e in range(experts):
            weights = router_ref[e : e + 1, pl.ds(own_half, half)].astype(f32)
            stat = jnp.where(lanes == e, jnp.sum(scaled * weights, axis=1, keepdims=True), stat)
        stat_own[micro] = stat
        stat_copy(micro).start()

    def prepare(side, source, micro, group, start):
        for u in range(*group):
            at = pl.ds(u * unit, unit)
            x = source[micro, :, :, pl.ds(u * pack, unit)].reshape(plan.main_rows, unit).astype(f32)
            if plan.rem:
                rest = source[micro, :, :, pl.ds(u * pack + unit, lane)]
                rest = dot(to_rows, rest.reshape(n_pair * tile_rows, lane))
                rest = [
                    rest[t * plan.rem_rows : (t + 1) * plan.rem_rows] for t in range(plan.tiles)
                ]
                x = jnp.concatenate([x, jnp.concatenate(rest, axis=1)], axis=0)
            square = x * x
            ssq[...] += functools.reduce(
                lambda a, b: a + b,
                [square[:, t * lane : (t + 1) * lane] for t in range(plan.tiles)],
            )
            gain = gain_ref[:, pl.ds(pl.multiple_of(start + u * unit, lane), unit)]
            lhs[side, :, at] = (x * gain).astype(bf16)

    def project(side, group, start):
        size = (group[1] - group[0]) * unit
        block = lhs[side, :, cols(group)]
        where = pl.ds(pl.multiple_of(start + group[0] * unit, lane), size)
        acc_g[...] += dot(block, wg[where, :])
        acc_u[...] += dot(block, wu[where, :])

    def gather(micro):
        ssq[...] = jnp.zeros_like(ssq)
        acc_g[...] = jnp.zeros_like(acc_g)
        acc_u[...] = jnp.zeros_like(acc_u)

        def from_partner(g):
            fwd_copy(micro, g).wait_recv()
            prepare(1, dpart, micro, groups[g], par_half)
            project(1, groups[g], par_half)

        for g, group in enumerate(groups):
            for rel in range(1, n_pair):
                disp_copy(micro, g, rel).wait_recv()
            fwd_copy(micro, g).start()
            prepare(0, drecv, micro, group, own_half)

            if g == 0:

                @pl.when(micro == 0)
                def _():
                    weight_copies[0].wait()
                    weight_copies[1].wait()

            project(0, group, own_half)
            if g > 0:
                from_partner(g - 1)
        from_partner(len(groups) - 1)

    def experts_out(micro):
        @pl.when(micro >= 2)
        def _():
            hid_copy(micro).wait_send()
            for g in range(len(groups)):
                for rel in range(1, n_pair):
                    comb_copy(micro, g, rel).wait_send()

        mean_square = jnp.sum(ssq[...], axis=1, keepdims=True) / plan.width
        scale = lax.rsqrt(mean_square + norm_epsilon)
        gate = acc_g[...] * scale
        hid_own[micro % 2] = (gate / (1.0 + jnp.exp(-gate)) * (acc_u[...] * scale)).astype(bf16)
        hid_copy(micro).start()

        @pl.when(micro == 0)
        def _():
            weight_copies[2].wait()

        own_rows = pl.ds(pl.multiple_of(core * plan.hid, plan.hid), plan.hid)
        par_rows = pl.ds(pl.multiple_of((1 - core) * plan.hid, plan.hid), plan.hid)
        mine = hid_own[micro % 2]
        for group in groups:
            acc_d[:, cols(group)] = dot(mine, wd[own_rows, cols(group)])
        hid_copy(micro).wait_recv()
        theirs = hid_par[micro]
        for g, group in enumerate(groups):
            value = acc_d[:, cols(group)] + dot(theirs, wd[par_rows, cols(group)])
            value = value.astype(bf16)
            for u in range(*group):
                at = (u - group[0]) * unit
                csend[micro % 2, :, :, pl.ds(u * pack, unit)] = value[
                    : plan.main_rows, at : at + unit
                ].reshape(n_pair, plan.main, unit)
                if plan.rem:
                    stacked = jnp.concatenate(
                        [
                            value[plan.main_rows :, at + t * lane : at + (t + 1) * lane]
                            for t in range(plan.tiles)
                        ],
                        axis=0,
                    )
                    csend[micro % 2, :, :, pl.ds(u * pack + unit, lane)] = (
                        dot(to_tiles, stacked).astype(bf16).reshape(n_pair, tile_rows, lane)
                    )
            for rel in range(1, n_pair):
                comb_copy(micro, g, rel).start()
            crecv[micro, pair, :, pack_cols(group)] = csend[micro % 2, pair, :, pack_cols(group)]

    def update(micro):
        stat_copy(micro).wait_recv()
        stat = stat_own[micro] + stat_par[micro]
        scale = lax.rsqrt(stat[:, experts : experts + 1] / plan.width + norm_epsilon)
        score = jax.nn.sigmoid(stat * scale)
        lanes = lax.broadcasted_iota(jnp.int32, (pair_rows, lane), 1)
        names = targets[micro]
        picked = [
            jnp.sum(jnp.where(lanes == names[:, k : k + 1], score, 0.0), axis=1, keepdims=True)
            for k in range(top)
        ]
        total = functools.reduce(lambda a, b: a + b, picked)
        mixing = [routed_scale * value / total for value in picked]
        for g, group in enumerate(groups):
            for rel in range(1, n_pair):
                comb_copy(micro, g, rel).wait_recv()
            for u in range(*group):
                main = crecv[micro, :, :, pl.ds(u * pack, unit)].reshape(plan.lanes_main, unit)
                out = dot(place_main[micro], main)
                if plan.rem:
                    rest = crecv[micro, :, :, pl.ds(u * pack + unit, lane)]
                    rest = dot(place_rem[micro], rest.reshape(plan.lanes_rem, lane))
                    each = top * pair_rows
                    out = out + jnp.concatenate(
                        [rest[t * each : (t + 1) * each] for t in range(plan.tiles)], axis=1
                    )
                x = xs[micro, :, pl.ds(u * unit, unit)].astype(f32)
                for k in range(top):
                    x = x + mixing[k] * out[k * pair_rows : (k + 1) * pair_rows]
                xs[micro, :, pl.ds(u * unit, unit)] = x.astype(bf16)

            @pl.when(section < last)
            def _():
                relay_copy(micro, g).start()

            @pl.when(jnp.logical_and(section == last, micro < micros - 1))
            def _():
                for block in range(2):
                    final_copy(micro, g, block).start()

            @pl.when(jnp.logical_and(section == last, micro == micros - 1))
            def _():
                final_partner_copy(g).start()
                fin[:, fin_cols(own_half, g)] = xs[
                    micro, pl.ds(own_block, rows), cols(group)
                ]

    def step(turn, unused):
        @pl.when(turn > 0)
        def _():
            experts_out(turn - 1)

        @pl.when(turn < micros)
        def _():
            dispatch(turn)
            statistics(turn)

        @pl.when(turn > 0)
        def _():
            update(turn - 1)

        @pl.when(turn < micros)
        def _():
            gather(turn)

        return unused

    lax.fori_loop(0, micros + 1, step, 0)

    for micro in range(max(0, micros - 2), micros):
        hid_copy(micro).wait_send()
        for g in range(len(groups)):
            for rel in range(1, n_pair):
                disp_copy(micro, g, rel).wait_send()
                comb_copy(micro, g, rel).wait_send()
    for micro in range(micros):
        stat_copy(micro).wait_send()
        for g in range(len(groups)):
            fwd_copy(micro, g).wait_send()

    def final_arrival(source, g):
        remote(
            fin.at[:, fin_cols(source * half, g)], fin.at[:, fin_cols(source * half, g)],
            fin_send.at[0, g, 0], fin_recv.at[source, g], partner,
        ).wait_recv()

    @pl.when(section < last)
    def _():
        for g in range(len(groups)):
            for micro in range(micros):
                relay_copy(micro, g).wait_send()
            for source in range(2):
                final_arrival(source, g)

    @pl.when(section == last)
    def _():
        for g in range(len(groups)):
            for micro in range(micros - 1):
                for block in range(2):
                    final_copy(micro, g, block).wait_send()
            final_partner_copy(g).wait_send()
            final_arrival(1 - core, g)

    out_ref[0] = fin[...]


def on_device(inputs, norm_gain, router_weight, gate_weight, up_weight, down_weight, routing):
    micros, rows, width = inputs.shape
    experts, top, hid = router_weight.shape[2], routing.shape[3], gate_weight.shape[2]
    plan = Plan(
        lax.axis_size("pp"), lax.axis_size("ep"), micros, rows, width, experts, top, hid
    )
    n_pair, count, half = plan.n_pair, len(plan.groups), plan.half
    packed = plan.units * plan.pack
    dma, vmem = pltpu.SemaphoreType.DMA, pltpu.VMEM
    any_spec = pl.BlockSpec(memory_space=pl.ANY)
    vmem_spec = pl.BlockSpec(memory_space=pltpu.VMEM)
    picks = plan.lanes_rem if plan.rem else 16
    return pl.pallas_call(
        functools.partial(kernel, plan),
        out_shape=jax.ShapeDtypeStruct((1, rows, width), bf16),
        in_specs=[any_spec, vmem_spec, vmem_spec, any_spec, any_spec, any_spec, vmem_spec],
        out_specs=vmem_spec,
        scratch_shapes=[
            vmem((2, micros, top, rows), jnp.int32),
            vmem((micros, plan.pair_rows, half), bf16),
            vmem((rows, width), bf16),
            vmem((2, n_pair, plan.main, packed), bf16),
            vmem((micros, n_pair, plan.main, packed), bf16),
            vmem((micros, n_pair, plan.main, packed), bf16),
            vmem((2, n_pair, plan.main, packed), bf16),
            vmem((micros, n_pair, plan.main, packed), bf16),
            vmem((width, hid), bf16),
            vmem((width, hid), bf16),
            vmem((2 * hid, half), bf16),
            vmem((2, plan.work_rows, half), bf16),
            vmem((plan.work_rows, lane), f32),
            vmem((plan.work_rows, hid), f32),
            vmem((plan.work_rows, hid), f32),
            vmem((plan.work_rows, half), f32),
            vmem((2, plan.work_rows, hid), bf16),
            vmem((micros, plan.work_rows, hid), bf16),
            vmem((micros, plan.pair_rows, lane), f32),
            vmem((micros, plan.pair_rows, lane), f32),
            vmem((micros, plan.lanes_main, plan.pair_rows), bf16),
            vmem((micros, picks, plan.tiles * plan.pair_rows), bf16),
            vmem((micros, top * plan.pair_rows, plan.lanes_main), bf16),
            vmem((micros, plan.tiles * top * plan.pair_rows, picks), bf16),
            vmem((micros, plan.pair_rows, lane), jnp.int32),
            dma((3,)), dma((micros,)), dma, dma, dma((micros,)), dma((micros,)),
            dma((2, count, n_pair)), dma((micros, count, n_pair)),
            dma((micros, count)), dma((micros, count)), dma((2,)), dma((micros,)),
            dma((2, count, n_pair)), dma((micros, count, n_pair)),
            dma((micros,)), dma((micros,)), dma((micros, count)), dma((micros, count)),
            dma((micros, count, 2)), dma((2, count)),
        ],
        compiler_params=pltpu.CompilerParams(
            collective_id=0, has_side_effects=True, vmem_limit_bytes=60 * 1024 * 1024
        ),
    )(
        inputs, norm_gain, router_weight[0].T, gate_weight, up_weight, down_weight,
        jnp.transpose(routing[0], (0, 2, 1)),
    )


def solution(mesh):
    return jax.shard_map(
        on_device,
        mesh=mesh,
        in_specs=(
            P(None, "ep", None),
            P("pp", None),
            P("pp", None, None),
            P("pp", None, "ep"),
            P("pp", None, "ep"),
            P("pp", None, "ep"),
            P("pp", None, "ep", None),
        ),
        out_specs=P("pp", "ep", None),
        check_vma=False,
    )
```

```python
import functools

import jax
import jax.numpy as jnp
from jax import lax
from jax.experimental import pallas as pl
from jax.experimental.pallas import tpu as pltpu
from jax.sharding import PartitionSpec as P

routed_scale = 2.5
norm_epsilon = 1e-06
lane = 128
tile_rows = 16
f32, bf16 = jnp.float32, jnp.bfloat16


class Plan:
    def __init__(self, n_pp, n_ep, micros, rows, width, experts, top, hid):
        self.n_pp, self.n_ep, self.n_pair = n_pp, n_ep, n_ep // 2
        self.micros, self.rows, self.width = micros, rows, width
        self.experts, self.top, self.hid = experts, top, hid
        self.half = width // 2
        self.pair_rows = 2 * rows
        most = rows * top * 5 // (4 * experts)
        slots = 2 * most
        main = tile_rows * max(1, slots // tile_rows)
        extra = max(0, slots - main)
        if extra > tile_rows // 2:
            main, extra = main + tile_rows, 0
        self.main = main
        self.rem = 0 if extra == 0 else (4 if extra <= 4 else 8)
        self.tiles = tile_rows // self.rem if self.rem else 4
        self.unit = lane * self.tiles
        self.pack = self.unit + (lane if self.rem else 0)
        self.units = self.half // self.unit
        self.main_rows = self.n_pair * self.main
        self.rem_rows = self.n_pair * self.rem
        self.work_rows = self.main_rows + self.rem_rows
        self.lanes_main = experts * self.main
        self.lanes_rem = experts * tile_rows
        count = min(4, self.units)
        cuts = [-(-self.units * g // count) for g in range(count + 1)]
        self.groups = list(zip(cuts[:-1], cuts[1:]))


def kernel(
    plan,
    inputs_hbm, gain_ref, router_ref, gate_hbm, up_hbm, down_hbm, routing_ref,
    out_ref,
    routes, xs, fin, dsend, drecv, dpart, csend, crecv, wg, wu, wd,
    lhs, ssq, acc_g, acc_u, acc_d, hid_own, hid_par, stat_own, stat_par,
    pick_main, pick_rem, place_main, place_rem, targets, mixing,
    weight_sem, init_sem, route_send, route_recv, init_send, init_recv,
    disp_send, disp_recv, fwd_send, fwd_recv, hid_send, hid_recv,
    comb_send, comb_recv, stat_send, stat_recv, relay_send, relay_recv, fin_send, fin_recv,
):
    section = lax.axis_index("pp")
    me = lax.axis_index("ep")
    core, pair = me % 2, me // 2
    last = plan.n_pp - 1
    n_pair, rows, half, unit, pack = plan.n_pair, plan.rows, plan.half, plan.unit, plan.pack
    pair_rows, experts, top = plan.pair_rows, plan.experts, plan.top
    groups = plan.groups
    micros = plan.micros
    own_half = pl.multiple_of(core * half, lane)
    par_half = pl.multiple_of((1 - core) * half, lane)
    own_block = pl.multiple_of(core * rows, rows)
    partner = {"ep": me + 1 - 2 * core}

    def flip(value, mask):
        for b in range((n_pair - 1).bit_length()):
            if mask >> b & 1:
                value = value + (1 << b) - 2 * (1 << b) * ((value // (1 << b)) % 2)
        return value

    def remote(src, dst, send, recv, where):
        return pltpu.make_async_remote_copy(
            src_ref=src, dst_ref=dst, send_sem=send, recv_sem=recv,
            device_id=where, device_id_type=pl.DeviceIdType.MESH,
        )

    def dot(a, b):
        return jnp.dot(a, b, preferred_element_type=f32)

    weight_copies = [
        pltpu.make_async_copy(gate_hbm.at[0], wg, weight_sem.at[0]),
        pltpu.make_async_copy(up_hbm.at[0], wu, weight_sem.at[1]),
        pltpu.make_async_copy(down_hbm.at[0], wd, weight_sem.at[2]),
    ]

    def init_local(micro):
        return pltpu.make_async_copy(
            inputs_hbm.at[micro, :, pl.ds(own_half, half)],
            xs.at[micro, pl.ds(own_block, rows), :], init_sem.at[micro],
        )

    def init_copy(micro):
        return remote(
            inputs_hbm.at[micro, :, pl.ds(par_half, half)],
            xs.at[micro, pl.ds(own_block, rows), :],
            init_send.at[micro], init_recv.at[micro], partner,
        )

    route_copy = remote(routing_ref, routes.at[core], route_send, route_recv, partner)

    def cols(group):
        return pl.ds(group[0] * unit, (group[1] - group[0]) * unit)

    def pack_cols(group):
        return pl.ds(group[0] * pack, (group[1] - group[0]) * pack)

    def disp_copy(micro, g, rel):
        to = flip(pair, rel)
        return remote(
            dsend.at[micro % 2, to, :, pack_cols(groups[g])],
            drecv.at[micro, pair, :, pack_cols(groups[g])],
            disp_send.at[micro % 2, g, rel], disp_recv.at[micro, g, rel],
            {"ep": 2 * to + core},
        )

    def fwd_copy(micro, g):
        return remote(
            drecv.at[micro, :, :, pack_cols(groups[g])],
            dpart.at[micro, :, :, pack_cols(groups[g])],
            fwd_send.at[micro, g], fwd_recv.at[micro, g], partner,
        )

    def hid_copy(micro):
        return remote(
            hid_own.at[micro % 2], hid_par.at[micro], hid_send.at[micro % 2], hid_recv.at[micro],
            partner,
        )

    def comb_copy(micro, g, rel):
        to = flip(pair, rel)
        return remote(
            csend.at[micro % 2, to, :, pack_cols(groups[g])],
            crecv.at[micro, pair, :, pack_cols(groups[g])],
            comb_send.at[micro % 2, g, rel], comb_recv.at[micro, g, rel],
            {"ep": 2 * to + core},
        )

    def stat_copy(micro):
        return remote(
            stat_own.at[micro], stat_par.at[micro], stat_send.at[micro], stat_recv.at[micro], partner
        )

    def relay_copy(micro, g):
        ref = xs.at[micro, :, cols(groups[g])]
        return remote(
            ref, ref, relay_send.at[micro, g], relay_recv.at[micro, g],
            {"pp": (section + 1) % plan.n_pp},
        )

    def fin_cols(half_start, g):
        start = pl.multiple_of(half_start + groups[g][0] * unit, lane)
        return pl.ds(start, (groups[g][1] - groups[g][0]) * unit)

    def final_copy(micro, g, block):
        return remote(
            xs.at[micro, pl.ds(block * rows, rows), cols(groups[g])],
            fin.at[:, fin_cols(own_half, g)],
            fin_send.at[micro, g, block], fin_recv.at[core, g],
            {"pp": micro, "ep": 2 * pair + block},
        )

    def final_partner_copy(g):
        return remote(
            xs.at[micros - 1, pl.ds(pl.multiple_of((1 - core) * rows, rows), rows), cols(groups[g])],
            fin.at[:, fin_cols(own_half, g)],
            fin_send.at[micros - 1, g, 0], fin_recv.at[core, g], partner,
        )

    @pl.when(section == 0)
    def _():
        for micro in range(micros):
            init_local(micro).start()

    barrier = pltpu.get_barrier_semaphore()
    greeted = [{"ep": 2 * flip(pair, rel) + core} for rel in range(1, n_pair)] + [partner]
    for step in range(1, plan.n_pp):
        other = (section + step) % plan.n_pp
        greeted += [{"pp": other}, {"pp": other, "ep": me + 1 - 2 * core}]
    for device in greeted:
        pl.semaphore_signal(barrier, inc=1, device_id=device, device_id_type=pl.DeviceIdType.MESH)
    pl.semaphore_wait(barrier, len(greeted))

    route_copy.start()

    @pl.when(section == 0)
    def _():
        for micro in range(micros):
            init_copy(micro).start()

    for copy in weight_copies:
        copy.start()

    routes[core] = routing_ref[...]
    route_copy.wait()

    def make_selections(micro, unused):
        names = jnp.concatenate([routes[0, micro], routes[1, micro]], axis=1)
        expert = lax.broadcasted_iota(jnp.int32, (experts, pair_rows), 0)
        hit = [expert == names[k : k + 1] for k in range(top)]
        chosen = functools.reduce(jnp.logical_or, hit)
        before = lax.broadcasted_iota(jnp.int32, (pair_rows, pair_rows), 0)
        after = lax.broadcasted_iota(jnp.int32, (pair_rows, pair_rows), 1)
        rank = dot(
            jnp.where(chosen, 1.0, 0.0).astype(bf16),
            jnp.where(before < after, 1.0, 0.0).astype(bf16),
        )
        main_target, rem_target, columns = [], [], []
        lanes = lax.broadcasted_iota(jnp.int32, (pair_rows, lane), 1)
        kept = jnp.zeros((pair_rows, lane), jnp.int32)
        for k in range(top):
            slot = jnp.sum(jnp.where(hit[k], rank, 0.0), axis=0, keepdims=True).astype(jnp.int32)
            name = names[k : k + 1]
            main_target.append(jnp.where(slot < plan.main, name * plan.main + slot, -1))
            rem_target.append(
                jnp.where(slot >= plan.main, name * tile_rows + slot - plan.main, -tile_rows * experts)
            )

            def column(row):
                return jnp.sum(
                    jnp.where(before == after, row, 0).astype(f32), axis=1, keepdims=True
                ).astype(jnp.int32)

            columns.append((column(main_target[k]), column(rem_target[k])))
            kept = jnp.where(lanes == k, column(name), kept)
        targets[micro] = kept
        spot = lax.broadcasted_iota(jnp.int32, (plan.lanes_main, pair_rows), 0)
        picks = functools.reduce(jnp.logical_or, [spot == target for target in main_target])
        pick_main[micro] = jnp.where(picks, 1.0, 0.0).astype(bf16)
        spot = lax.broadcasted_iota(jnp.int32, (pair_rows, plan.lanes_main), 1)
        place_main[micro] = jnp.concatenate(
            [jnp.where(spot == columns[k][0], 1.0, 0.0) for k in range(top)], axis=0
        ).astype(bf16)
        if plan.rem:
            spot = lax.broadcasted_iota(jnp.int32, (plan.lanes_rem, pair_rows), 0)
            pick_rem[micro] = jnp.concatenate(
                [
                    jnp.where(
                        functools.reduce(
                            jnp.logical_or, [spot == target + t * plan.rem for target in rem_target]
                        ),
                        1.0, 0.0,
                    )
                    for t in range(plan.tiles)
                ],
                axis=1,
            ).astype(bf16)
            spot = lax.broadcasted_iota(jnp.int32, (pair_rows, plan.lanes_rem), 1)
            place_rem[micro] = jnp.concatenate(
                [
                    jnp.where(spot == columns[k][1] + t * plan.rem, 1.0, 0.0)
                    for t in range(plan.tiles)
                    for k in range(top)
                ],
                axis=0,
            ).astype(bf16)
        return unused

    lax.fori_loop(0, micros, make_selections, 0)

    if plan.rem:
        size = n_pair * tile_rows
        row = lax.broadcasted_iota(jnp.int32, (size, size), 0)
        column = lax.broadcasted_iota(jnp.int32, (size, size), 1)
        rem, tiles = plan.rem, plan.tiles

        def by_tile(index):
            tile, rest = index // (n_pair * rem), index % (n_pair * rem)
            return (rest // rem) * tile_rows + tile * rem + rest % rem

        to_rows = jnp.where(by_tile(row) == column, 1.0, 0.0).astype(bf16)
        to_tiles = jnp.where(by_tile(column) == row, 1.0, 0.0).astype(bf16)

    def dispatch_begin(micro):
        @pl.when(micro >= 2)
        def _():
            for g in range(len(groups)):
                for rel in range(1, n_pair):
                    disp_copy(micro, g, rel).wait_send()

        @pl.when(section == 0)
        def _():
            init_local(micro).wait()
            init_copy(micro).wait()

    def dispatch(micro, g):
        group, pick = groups[g], pick_main[micro]

        @pl.when(section > 0)
        def _():
            relay_copy(micro, g).wait_recv()

        for u in range(*group):
            x = xs[micro, :, pl.ds(u * unit, unit)]
            packed = dot(pick, x).astype(bf16)
            dsend[micro % 2, :, :, pl.ds(u * pack, unit)] = packed.reshape(
                experts, plan.main, unit
            )
            if plan.rem:
                stacked = jnp.concatenate(
                    [x[:, t * lane : (t + 1) * lane] for t in range(plan.tiles)], axis=0
                )
                packed = dot(pick_rem[micro], stacked).astype(bf16)
                dsend[micro % 2, :, :, pl.ds(u * pack + unit, lane)] = packed.reshape(
                    experts, tile_rows, lane
                )
        for rel in reversed(range(1, n_pair)):
            disp_copy(micro, g, rel).start()
        drecv[micro, pair, :, pack_cols(group)] = dsend[micro % 2, pair, :, pack_cols(group)]

    def statistics(micro):
        x = xs[micro].astype(f32)
        lanes = lax.broadcasted_iota(jnp.int32, (pair_rows, lane), 1)
        stat = jnp.where(lanes == experts, jnp.sum(x * x, axis=1, keepdims=True), 0.0)
        scaled = x * gain_ref[:, pl.ds(own_half, half)]
        for e in range(experts):
            weights = router_ref[e : e + 1, pl.ds(own_half, half)].astype(f32)
            stat = jnp.where(lanes == e, jnp.sum(scaled * weights, axis=1, keepdims=True), stat)
        stat_own[micro] = stat
        stat_copy(micro).start()

    def prepare(side, source, micro, group, start):
        for u in range(*group):
            at = pl.ds(u * unit, unit)
            x = source[micro, :, :, pl.ds(u * pack, unit)].reshape(plan.main_rows, unit).astype(f32)
            if plan.rem:
                rest = source[micro, :, :, pl.ds(u * pack + unit, lane)]
                rest = dot(to_rows, rest.reshape(n_pair * tile_rows, lane))
                rest = [
                    rest[t * plan.rem_rows : (t + 1) * plan.rem_rows] for t in range(plan.tiles)
                ]
                x = jnp.concatenate([x, jnp.concatenate(rest, axis=1)], axis=0)
            square = x * x
            ssq[...] += functools.reduce(
                lambda a, b: a + b,
                [square[:, t * lane : (t + 1) * lane] for t in range(plan.tiles)],
            )
            gain = gain_ref[:, pl.ds(pl.multiple_of(start + u * unit, lane), unit)]
            lhs[side, :, at] = (x * gain).astype(bf16)

    def project(side, group, start):
        size = (group[1] - group[0]) * unit
        block = lhs[side, :, cols(group)]
        where = pl.ds(pl.multiple_of(start + group[0] * unit, lane), size)
        acc_g[...] += dot(block, wg[where, :])
        acc_u[...] += dot(block, wu[where, :])

    def gather(micro):
        ssq[...] = jnp.zeros_like(ssq)
        acc_g[...] = jnp.zeros_like(acc_g)
        acc_u[...] = jnp.zeros_like(acc_u)

        def from_partner(g):
            fwd_copy(micro, g).wait_recv()
            prepare(1, dpart, micro, groups[g], par_half)
            project(1, groups[g], par_half)

        for g, group in enumerate(groups):
            for rel in range(1, n_pair):
                disp_copy(micro, g, rel).wait_recv()
            fwd_copy(micro, g).start()
            prepare(0, drecv, micro, group, own_half)

            if g == 0:

                @pl.when(micro == 0)
                def _():
                    weight_copies[0].wait()
                    weight_copies[1].wait()

            project(0, group, own_half)
            if g > 0:
                from_partner(g - 1)
        from_partner(len(groups) - 1)

    def experts_out(micro):
        @pl.when(micro >= 2)
        def _():
            hid_copy(micro).wait_send()
            for g in range(len(groups)):
                for rel in range(1, n_pair):
                    comb_copy(micro, g, rel).wait_send()

        mean_square = jnp.sum(ssq[...], axis=1, keepdims=True) / plan.width
        scale = lax.rsqrt(mean_square + norm_epsilon)
        gate = acc_g[...] * scale
        hid_own[micro % 2] = (gate / (1.0 + jnp.exp(-gate)) * (acc_u[...] * scale)).astype(bf16)
        hid_copy(micro).start()

        @pl.when(micro == 0)
        def _():
            weight_copies[2].wait()

        own_rows = pl.ds(pl.multiple_of(core * plan.hid, plan.hid), plan.hid)
        par_rows = pl.ds(pl.multiple_of((1 - core) * plan.hid, plan.hid), plan.hid)
        mine = hid_own[micro % 2]
        for group in groups:
            acc_d[:, cols(group)] = dot(mine, wd[own_rows, cols(group)])
        hid_copy(micro).wait_recv()
        theirs = hid_par[micro]
        for g, group in enumerate(groups):
            value = acc_d[:, cols(group)] + dot(theirs, wd[par_rows, cols(group)])
            value = value.astype(bf16)
            for u in range(*group):
                at = (u - group[0]) * unit
                csend[micro % 2, :, :, pl.ds(u * pack, unit)] = value[
                    : plan.main_rows, at : at + unit
                ].reshape(n_pair, plan.main, unit)
                if plan.rem:
                    stacked = jnp.concatenate(
                        [
                            value[plan.main_rows :, at + t * lane : at + (t + 1) * lane]
                            for t in range(plan.tiles)
                        ],
                        axis=0,
                    )
                    csend[micro % 2, :, :, pl.ds(u * pack + unit, lane)] = (
                        dot(to_tiles, stacked).astype(bf16).reshape(n_pair, tile_rows, lane)
                    )
            for rel in reversed(range(1, n_pair)):
                comb_copy(micro, g, rel).start()
            crecv[micro, pair, :, pack_cols(group)] = csend[micro % 2, pair, :, pack_cols(group)]

    def mix(micro):
        stat_copy(micro).wait_recv()
        stat = stat_own[micro] + stat_par[micro]
        scale = lax.rsqrt(stat[:, experts : experts + 1] / plan.width + norm_epsilon)
        score = jax.nn.sigmoid(stat * scale)
        lanes = lax.broadcasted_iota(jnp.int32, (pair_rows, lane), 1)
        names = targets[micro]
        picked = [
            jnp.sum(jnp.where(lanes == names[:, k : k + 1], score, 0.0), axis=1, keepdims=True)
            for k in range(top)
        ]
        total = functools.reduce(lambda a, b: a + b, picked)
        for k in range(top):
            mixing[k] = jnp.broadcast_to(routed_scale * picked[k] / total, (pair_rows, lane))

    def update(micro, g):
        group = groups[g]
        for rel in range(1, n_pair):
            comb_copy(micro, g, rel).wait_recv()
        for u in range(*group):
            main = crecv[micro, :, :, pl.ds(u * pack, unit)].reshape(plan.lanes_main, unit)
            out = dot(place_main[micro], main)
            if plan.rem:
                rest = crecv[micro, :, :, pl.ds(u * pack + unit, lane)]
                rest = dot(place_rem[micro], rest.reshape(plan.lanes_rem, lane))
                each = top * pair_rows
                out = out + jnp.concatenate(
                    [rest[t * each : (t + 1) * each] for t in range(plan.tiles)], axis=1
                )
            x = xs[micro, :, pl.ds(u * unit, unit)].astype(f32)
            for k in range(top):
                x = x + mixing[k, :, :1] * out[k * pair_rows : (k + 1) * pair_rows]
            xs[micro, :, pl.ds(u * unit, unit)] = x.astype(bf16)

        @pl.when(section < last)
        def _():
            relay_copy(micro, g).start()

        @pl.when(jnp.logical_and(section == last, micro < micros - 1))
        def _():
            for block in range(2):
                final_copy(micro, g, block).start()

        @pl.when(jnp.logical_and(section == last, micro == micros - 1))
        def _():
            final_partner_copy(g).start()
            fin[:, fin_cols(own_half, g)] = xs[
                micro, pl.ds(own_block, rows), cols(group)
            ]

    def step(turn, unused):
        @pl.when(turn > 0)
        def _():
            experts_out(turn - 1)
            mix(turn - 1)

        @pl.when(turn < micros)
        def _():
            dispatch_begin(turn)

        for g in range(len(groups)):

            @pl.when(turn > 0)
            def _():
                update(turn - 1, g)

            @pl.when(turn < micros)
            def _():
                dispatch(turn, g)

        @pl.when(turn < micros)
        def _():
            statistics(turn)
            gather(turn)

        return unused

    lax.fori_loop(0, micros + 1, step, 0)

    for micro in range(max(0, micros - 2), micros):
        hid_copy(micro).wait_send()
        for g in range(len(groups)):
            for rel in range(1, n_pair):
                disp_copy(micro, g, rel).wait_send()
                comb_copy(micro, g, rel).wait_send()
    for micro in range(micros):
        stat_copy(micro).wait_send()
        for g in range(len(groups)):
            fwd_copy(micro, g).wait_send()

    def final_arrival(source, g):
        remote(
            fin.at[:, fin_cols(source * half, g)], fin.at[:, fin_cols(source * half, g)],
            fin_send.at[0, g, 0], fin_recv.at[source, g], partner,
        ).wait_recv()

    @pl.when(section < last)
    def _():
        for g in range(len(groups)):
            for micro in range(micros):
                relay_copy(micro, g).wait_send()
            for source in range(2):
                final_arrival(source, g)

    @pl.when(section == last)
    def _():
        for g in range(len(groups)):
            for micro in range(micros - 1):
                for block in range(2):
                    final_copy(micro, g, block).wait_send()
            final_partner_copy(g).wait_send()
            final_arrival(1 - core, g)

    out_ref[0] = fin[...]


def on_device(inputs, norm_gain, router_weight, gate_weight, up_weight, down_weight, routing):
    micros, rows, width = inputs.shape
    experts, top, hid = router_weight.shape[2], routing.shape[3], gate_weight.shape[2]
    plan = Plan(
        lax.axis_size("pp"), lax.axis_size("ep"), micros, rows, width, experts, top, hid
    )
    n_pair, count, half = plan.n_pair, len(plan.groups), plan.half
    packed = plan.units * plan.pack
    dma, vmem = pltpu.SemaphoreType.DMA, pltpu.VMEM
    any_spec = pl.BlockSpec(memory_space=pl.ANY)
    vmem_spec = pl.BlockSpec(memory_space=pltpu.VMEM)
    picks = plan.lanes_rem if plan.rem else 16
    return pl.pallas_call(
        functools.partial(kernel, plan),
        out_shape=jax.ShapeDtypeStruct((1, rows, width), bf16),
        in_specs=[any_spec, vmem_spec, vmem_spec, any_spec, any_spec, any_spec, vmem_spec],
        out_specs=vmem_spec,
        scratch_shapes=[
            vmem((2, micros, top, rows), jnp.int32),
            vmem((micros, plan.pair_rows, half), bf16),
            vmem((rows, width), bf16),
            vmem((2, n_pair, plan.main, packed), bf16),
            vmem((micros, n_pair, plan.main, packed), bf16),
            vmem((micros, n_pair, plan.main, packed), bf16),
            vmem((2, n_pair, plan.main, packed), bf16),
            vmem((micros, n_pair, plan.main, packed), bf16),
            vmem((width, hid), bf16),
            vmem((width, hid), bf16),
            vmem((2 * hid, half), bf16),
            vmem((2, plan.work_rows, half), bf16),
            vmem((plan.work_rows, lane), f32),
            vmem((plan.work_rows, hid), f32),
            vmem((plan.work_rows, hid), f32),
            vmem((plan.work_rows, half), f32),
            vmem((2, plan.work_rows, hid), bf16),
            vmem((micros, plan.work_rows, hid), bf16),
            vmem((micros, plan.pair_rows, lane), f32),
            vmem((micros, plan.pair_rows, lane), f32),
            vmem((micros, plan.lanes_main, plan.pair_rows), bf16),
            vmem((micros, picks, plan.tiles * plan.pair_rows), bf16),
            vmem((micros, top * plan.pair_rows, plan.lanes_main), bf16),
            vmem((micros, plan.tiles * top * plan.pair_rows, picks), bf16),
            vmem((micros, plan.pair_rows, lane), jnp.int32),
            vmem((top, plan.pair_rows, lane), f32),
            dma((3,)), dma((micros,)), dma, dma, dma((micros,)), dma((micros,)),
            dma((2, count, n_pair)), dma((micros, count, n_pair)),
            dma((micros, count)), dma((micros, count)), dma((2,)), dma((micros,)),
            dma((2, count, n_pair)), dma((micros, count, n_pair)),
            dma((micros,)), dma((micros,)), dma((micros, count)), dma((micros, count)),
            dma((micros, count, 2)), dma((2, count)),
        ],
        compiler_params=pltpu.CompilerParams(
            collective_id=0, has_side_effects=True, vmem_limit_bytes=60 * 1024 * 1024
        ),
    )(
        inputs, norm_gain, router_weight[0].T, gate_weight, up_weight, down_weight,
        jnp.transpose(routing[0], (0, 2, 1)),
    )


def solution(mesh):
    return jax.shard_map(
        on_device,
        mesh=mesh,
        in_specs=(
            P(None, "ep", None),
            P("pp", None),
            P("pp", None, None),
            P("pp", None, "ep"),
            P("pp", None, "ep"),
            P("pp", None, "ep"),
            P("pp", None, "ep", None),
        ),
        out_specs=P("pp", "ep", None),
        check_vma=False,
    )
```

```python
import functools

import jax
import jax.numpy as jnp
from jax import lax
from jax.experimental import pallas as pl
from jax.experimental.pallas import tpu as pltpu
from jax.sharding import PartitionSpec as P

routed_scale = 2.5
norm_epsilon = 1e-06
lane = 128
tile_rows = 16
f32, bf16 = jnp.float32, jnp.bfloat16


class Plan:
    def __init__(self, n_pp, n_ep, micros, rows, width, experts, top, hid):
        self.n_pp, self.n_ep, self.n_pair = n_pp, n_ep, n_ep // 2
        self.micros, self.rows, self.width = micros, rows, width
        self.experts, self.top, self.hid = experts, top, hid
        self.half = width // 2
        self.pair_rows = 2 * rows
        most = rows * top * 5 // (4 * experts)
        slots = 2 * most
        main = tile_rows * max(1, slots // tile_rows)
        extra = max(0, slots - main)
        if extra > tile_rows // 2:
            main, extra = main + tile_rows, 0
        self.main = main
        self.rem = 0 if extra == 0 else (4 if extra <= 4 else 8)
        self.tiles = tile_rows // self.rem if self.rem else 4
        self.unit = lane * self.tiles
        self.pack = self.unit + (lane if self.rem else 0)
        self.units = self.half // self.unit
        self.main_rows = self.n_pair * self.main
        self.rem_rows = self.n_pair * self.rem
        self.work_rows = self.main_rows + self.rem_rows
        self.lanes_main = experts * self.main
        self.lanes_rem = experts * tile_rows
        count = min(4, self.units)
        cuts = [-(-self.units * g // count) for g in range(count + 1)]
        self.groups = list(zip(cuts[:-1], cuts[1:]))


def kernel(
    plan,
    inputs_hbm, gain_ref, router_ref, gate_hbm, up_hbm, down_hbm, routing_ref,
    out_ref,
    routes, xs, fin, dsend, drecv, dpart, csend, crecv, wg, wu, wd,
    lhs, ssq, acc_g, acc_u, acc_d, hid_own, hid_par, stat_own, stat_par,
    pick_main, pick_rem, place_main, place_rem, targets, mixing,
    weight_sem, init_sem, route_send, route_recv, init_send, init_recv,
    disp_send, disp_recv, fwd_send, fwd_recv, hid_send, hid_recv,
    comb_send, comb_recv, stat_send, stat_recv, relay_send, relay_recv, fin_send, fin_recv,
):
    section = lax.axis_index("pp")
    me = lax.axis_index("ep")
    core, pair = me % 2, me // 2
    last = plan.n_pp - 1
    n_pair, rows, half, unit, pack = plan.n_pair, plan.rows, plan.half, plan.unit, plan.pack
    pair_rows, experts, top = plan.pair_rows, plan.experts, plan.top
    groups = plan.groups
    micros = plan.micros
    own_half = pl.multiple_of(core * half, lane)
    par_half = pl.multiple_of((1 - core) * half, lane)
    own_block = pl.multiple_of(core * rows, rows)
    partner = {"ep": me + 1 - 2 * core}

    def flip(value, mask):
        for b in range((n_pair - 1).bit_length()):
            if mask >> b & 1:
                value = value + (1 << b) - 2 * (1 << b) * ((value // (1 << b)) % 2)
        return value

    def remote(src, dst, send, recv, where):
        return pltpu.make_async_remote_copy(
            src_ref=src, dst_ref=dst, send_sem=send, recv_sem=recv,
            device_id=where, device_id_type=pl.DeviceIdType.MESH,
        )

    def dot(a, b):
        return jnp.dot(a, b, preferred_element_type=f32)

    weight_copies = [
        pltpu.make_async_copy(gate_hbm.at[0], wg, weight_sem.at[0]),
        pltpu.make_async_copy(up_hbm.at[0], wu, weight_sem.at[1]),
        pltpu.make_async_copy(down_hbm.at[0], wd, weight_sem.at[2]),
    ]

    def init_local(micro):
        return pltpu.make_async_copy(
            inputs_hbm.at[micro, :, pl.ds(own_half, half)],
            xs.at[micro, pl.ds(own_block, rows), :], init_sem.at[micro],
        )

    def init_copy(micro):
        return remote(
            inputs_hbm.at[micro, :, pl.ds(par_half, half)],
            xs.at[micro, pl.ds(own_block, rows), :],
            init_send.at[micro], init_recv.at[micro], partner,
        )

    route_copy = remote(routing_ref, routes.at[core], route_send, route_recv, partner)

    def cols(group):
        return pl.ds(group[0] * unit, (group[1] - group[0]) * unit)

    def pack_cols(group):
        return pl.ds(group[0] * pack, (group[1] - group[0]) * pack)

    def disp_copy(micro, g, rel):
        to = flip(pair, rel)
        return remote(
            dsend.at[micro % 2, to, :, pack_cols(groups[g])],
            drecv.at[micro, pair, :, pack_cols(groups[g])],
            disp_send.at[micro % 2, g, rel], disp_recv.at[micro, g, rel],
            {"ep": 2 * to + core},
        )

    def fwd_copy(micro, g):
        return remote(
            drecv.at[micro, :, :, pack_cols(groups[g])],
            dpart.at[micro, :, :, pack_cols(groups[g])],
            fwd_send.at[micro, g], fwd_recv.at[micro, g], partner,
        )

    def hid_copy(micro):
        return remote(
            hid_own.at[micro % 2], hid_par.at[micro], hid_send.at[micro % 2], hid_recv.at[micro],
            partner,
        )

    def comb_copy(micro, g, rel):
        to = flip(pair, rel)
        return remote(
            csend.at[micro % 2, to, :, pack_cols(groups[g])],
            crecv.at[micro, pair, :, pack_cols(groups[g])],
            comb_send.at[micro % 2, g, rel], comb_recv.at[micro, g, rel],
            {"ep": 2 * to + core},
        )

    def stat_copy(micro):
        return remote(
            stat_own.at[micro], stat_par.at[micro], stat_send.at[micro], stat_recv.at[micro], partner
        )

    def relay_copy(micro, g):
        ref = xs.at[micro, :, cols(groups[g])]
        return remote(
            ref, ref, relay_send.at[micro, g], relay_recv.at[micro, g],
            {"pp": (section + 1) % plan.n_pp},
        )

    def fin_cols(half_start, g):
        start = pl.multiple_of(half_start + groups[g][0] * unit, lane)
        return pl.ds(start, (groups[g][1] - groups[g][0]) * unit)

    def final_copy(micro, g, block):
        return remote(
            xs.at[micro, pl.ds(block * rows, rows), cols(groups[g])],
            fin.at[:, fin_cols(own_half, g)],
            fin_send.at[micro, g, block], fin_recv.at[core, g],
            {"pp": micro, "ep": 2 * pair + block},
        )

    def final_partner_copy(g):
        return remote(
            xs.at[micros - 1, pl.ds(pl.multiple_of((1 - core) * rows, rows), rows), cols(groups[g])],
            fin.at[:, fin_cols(own_half, g)],
            fin_send.at[micros - 1, g, 0], fin_recv.at[core, g], partner,
        )

    @pl.when(section == 0)
    def _():
        for micro in range(micros):
            init_local(micro).start()

    barrier = pltpu.get_barrier_semaphore()
    greeted = [{"ep": 2 * flip(pair, rel) + core} for rel in range(1, n_pair)] + [partner]
    for step in range(1, plan.n_pp):
        other = (section + step) % plan.n_pp
        greeted += [{"pp": other}, {"pp": other, "ep": me + 1 - 2 * core}]
    for device in greeted:
        pl.semaphore_signal(barrier, inc=1, device_id=device, device_id_type=pl.DeviceIdType.MESH)
    pl.semaphore_wait(barrier, len(greeted))

    route_copy.start()

    @pl.when(section == 0)
    def _():
        for micro in range(micros):
            init_copy(micro).start()

    for copy in weight_copies:
        copy.start()

    routes[core] = routing_ref[...]
    route_copy.wait()

    def make_selections(micro, unused):
        names = jnp.concatenate([routes[0, micro], routes[1, micro]], axis=1)
        expert = lax.broadcasted_iota(jnp.int32, (experts, pair_rows), 0)
        hit = [expert == names[k : k + 1] for k in range(top)]
        chosen = functools.reduce(jnp.logical_or, hit)
        before = lax.broadcasted_iota(jnp.int32, (pair_rows, pair_rows), 0)
        after = lax.broadcasted_iota(jnp.int32, (pair_rows, pair_rows), 1)
        rank = dot(
            jnp.where(chosen, 1.0, 0.0).astype(bf16),
            jnp.where(before < after, 1.0, 0.0).astype(bf16),
        )
        main_target, rem_target, columns = [], [], []
        lanes = lax.broadcasted_iota(jnp.int32, (pair_rows, lane), 1)
        kept = jnp.zeros((pair_rows, lane), jnp.int32)
        for k in range(top):
            slot = jnp.sum(jnp.where(hit[k], rank, 0.0), axis=0, keepdims=True).astype(jnp.int32)
            name = names[k : k + 1]
            main_target.append(jnp.where(slot < plan.main, name * plan.main + slot, -1))
            rem_target.append(
                jnp.where(slot >= plan.main, name * tile_rows + slot - plan.main, -tile_rows * experts)
            )

            def column(row):
                return jnp.sum(
                    jnp.where(before == after, row, 0).astype(f32), axis=1, keepdims=True
                ).astype(jnp.int32)

            columns.append((column(main_target[k]), column(rem_target[k])))
            kept = jnp.where(lanes == k, column(name), kept)
        targets[micro] = kept
        spot = lax.broadcasted_iota(jnp.int32, (plan.lanes_main, pair_rows), 0)
        picks = functools.reduce(jnp.logical_or, [spot == target for target in main_target])
        pick_main[micro] = jnp.where(picks, 1.0, 0.0).astype(bf16)
        spot = lax.broadcasted_iota(jnp.int32, (pair_rows, plan.lanes_main), 1)
        place_main[micro] = jnp.concatenate(
            [jnp.where(spot == columns[k][0], 1.0, 0.0) for k in range(top)], axis=0
        ).astype(bf16)
        if plan.rem:
            spot = lax.broadcasted_iota(jnp.int32, (plan.lanes_rem, pair_rows), 0)
            pick_rem[micro] = jnp.concatenate(
                [
                    jnp.where(
                        functools.reduce(
                            jnp.logical_or, [spot == target + t * plan.rem for target in rem_target]
                        ),
                        1.0, 0.0,
                    )
                    for t in range(plan.tiles)
                ],
                axis=1,
            ).astype(bf16)
            spot = lax.broadcasted_iota(jnp.int32, (pair_rows, plan.lanes_rem), 1)
            place_rem[micro] = jnp.concatenate(
                [
                    jnp.where(spot == columns[k][1] + t * plan.rem, 1.0, 0.0)
                    for t in range(plan.tiles)
                    for k in range(top)
                ],
                axis=0,
            ).astype(bf16)
        return unused

    lax.fori_loop(0, micros, make_selections, 0)

    if plan.rem:
        size = n_pair * tile_rows
        row = lax.broadcasted_iota(jnp.int32, (size, size), 0)
        column = lax.broadcasted_iota(jnp.int32, (size, size), 1)
        rem, tiles = plan.rem, plan.tiles

        def by_tile(index):
            tile, rest = index // (n_pair * rem), index % (n_pair * rem)
            return (rest // rem) * tile_rows + tile * rem + rest % rem

        to_rows = jnp.where(by_tile(row) == column, 1.0, 0.0).astype(bf16)
        to_tiles = jnp.where(by_tile(column) == row, 1.0, 0.0).astype(bf16)

    def dispatch_begin(micro):
        @pl.when(micro >= 2)
        def _():
            for g in range(len(groups)):
                for rel in range(1, n_pair):
                    disp_copy(micro, g, rel).wait_send()

        @pl.when(section == 0)
        def _():
            init_local(micro).wait()
            init_copy(micro).wait()

    def dispatch(micro, g):
        group, pick = groups[g], pick_main[micro]

        @pl.when(section > 0)
        def _():
            relay_copy(micro, g).wait_recv()

        for u in range(*group):
            x = xs[micro, :, pl.ds(u * unit, unit)]
            packed = dot(pick, x).astype(bf16)
            dsend[micro % 2, :, :, pl.ds(u * pack, unit)] = packed.reshape(
                experts, plan.main, unit
            )
            if plan.rem:
                stacked = jnp.concatenate(
                    [x[:, t * lane : (t + 1) * lane] for t in range(plan.tiles)], axis=0
                )
                packed = dot(pick_rem[micro], stacked).astype(bf16)
                dsend[micro % 2, :, :, pl.ds(u * pack + unit, lane)] = packed.reshape(
                    experts, tile_rows, lane
                )
        for rel in reversed(range(1, n_pair)):
            disp_copy(micro, g, rel).start()
        drecv[micro, pair, :, pack_cols(group)] = dsend[micro % 2, pair, :, pack_cols(group)]

    def statistics(micro):
        x = xs[micro].astype(f32)
        lanes = lax.broadcasted_iota(jnp.int32, (pair_rows, lane), 1)
        stat = jnp.where(lanes == experts, jnp.sum(x * x, axis=1, keepdims=True), 0.0)
        scaled = x * gain_ref[:, pl.ds(own_half, half)]
        for e in range(experts):
            weights = router_ref[e : e + 1, pl.ds(own_half, half)].astype(f32)
            stat = jnp.where(lanes == e, jnp.sum(scaled * weights, axis=1, keepdims=True), stat)
        stat_own[micro] = stat
        stat_copy(micro).start()

    def prepare(side, source, micro, group, start):
        for u in range(*group):
            at = pl.ds(u * unit, unit)
            x = source[micro, :, :, pl.ds(u * pack, unit)].reshape(plan.main_rows, unit).astype(f32)
            if plan.rem:
                rest = source[micro, :, :, pl.ds(u * pack + unit, lane)]
                rest = dot(to_rows, rest.reshape(n_pair * tile_rows, lane))
                rest = [
                    rest[t * plan.rem_rows : (t + 1) * plan.rem_rows] for t in range(plan.tiles)
                ]
                x = jnp.concatenate([x, jnp.concatenate(rest, axis=1)], axis=0)
            square = x * x
            ssq[...] += functools.reduce(
                lambda a, b: a + b,
                [square[:, t * lane : (t + 1) * lane] for t in range(plan.tiles)],
            )
            gain = gain_ref[:, pl.ds(pl.multiple_of(start + u * unit, lane), unit)]
            lhs[side, :, at] = (x * gain).astype(bf16)

    def project(side, group, start):
        size = (group[1] - group[0]) * unit
        block = lhs[side, :, cols(group)]
        where = pl.ds(pl.multiple_of(start + group[0] * unit, lane), size)
        acc_g[...] += dot(block, wg[where, :])
        acc_u[...] += dot(block, wu[where, :])

    def gather_begin():
        ssq[...] = jnp.zeros_like(ssq)
        acc_g[...] = jnp.zeros_like(acc_g)
        acc_u[...] = jnp.zeros_like(acc_u)

    def from_partner(micro, g):
        fwd_copy(micro, g).wait_recv()
        prepare(1, dpart, micro, groups[g], par_half)
        project(1, groups[g], par_half)

    def gather(micro, g):
        for rel in range(1, n_pair):
            disp_copy(micro, g, rel).wait_recv()
        fwd_copy(micro, g).start()
        prepare(0, drecv, micro, groups[g], own_half)

        if g == 0:

            @pl.when(micro == 0)
            def _():
                weight_copies[0].wait()
                weight_copies[1].wait()

        project(0, groups[g], own_half)
        if g > 0:
            from_partner(micro, g - 1)

    own_rows = pl.ds(pl.multiple_of(core * plan.hid, plan.hid), plan.hid)
    par_rows = pl.ds(pl.multiple_of((1 - core) * plan.hid, plan.hid), plan.hid)

    def experts_begin(micro):
        @pl.when(micro >= 2)
        def _():
            hid_copy(micro).wait_send()
            for g in range(len(groups)):
                for rel in range(1, n_pair):
                    comb_copy(micro, g, rel).wait_send()

        mean_square = jnp.sum(ssq[...], axis=1, keepdims=True) / plan.width
        scale = lax.rsqrt(mean_square + norm_epsilon)
        gate = acc_g[...] * scale
        hid_own[micro % 2] = (gate / (1.0 + jnp.exp(-gate)) * (acc_u[...] * scale)).astype(bf16)
        hid_copy(micro).start()

        @pl.when(micro == 0)
        def _():
            weight_copies[2].wait()

        mine = hid_own[micro % 2]
        for group in groups:
            acc_d[:, cols(group)] = dot(mine, wd[own_rows, cols(group)])

    def experts_finish(micro, g):
        group = groups[g]
        if g == 0:
            hid_copy(micro).wait_recv()
        value = acc_d[:, cols(group)] + dot(hid_par[micro], wd[par_rows, cols(group)])
        value = value.astype(bf16)
        for u in range(*group):
            at = (u - group[0]) * unit
            csend[micro % 2, :, :, pl.ds(u * pack, unit)] = value[
                : plan.main_rows, at : at + unit
            ].reshape(n_pair, plan.main, unit)
            if plan.rem:
                stacked = jnp.concatenate(
                    [
                        value[plan.main_rows :, at + t * lane : at + (t + 1) * lane]
                        for t in range(plan.tiles)
                    ],
                    axis=0,
                )
                csend[micro % 2, :, :, pl.ds(u * pack + unit, lane)] = (
                    dot(to_tiles, stacked).astype(bf16).reshape(n_pair, tile_rows, lane)
                )
        for rel in reversed(range(1, n_pair)):
            comb_copy(micro, g, rel).start()
        crecv[micro, pair, :, pack_cols(group)] = csend[micro % 2, pair, :, pack_cols(group)]

    def mix(micro):
        stat_copy(micro).wait_recv()
        stat = stat_own[micro] + stat_par[micro]
        scale = lax.rsqrt(stat[:, experts : experts + 1] / plan.width + norm_epsilon)
        score = jax.nn.sigmoid(stat * scale)
        lanes = lax.broadcasted_iota(jnp.int32, (pair_rows, lane), 1)
        names = targets[micro]
        picked = [
            jnp.sum(jnp.where(lanes == names[:, k : k + 1], score, 0.0), axis=1, keepdims=True)
            for k in range(top)
        ]
        total = functools.reduce(lambda a, b: a + b, picked)
        for k in range(top):
            mixing[k] = jnp.broadcast_to(routed_scale * picked[k] / total, (pair_rows, lane))

    def update(micro, g):
        group = groups[g]
        for rel in range(1, n_pair):
            comb_copy(micro, g, rel).wait_recv()
        for u in range(*group):
            main = crecv[micro, :, :, pl.ds(u * pack, unit)].reshape(plan.lanes_main, unit)
            out = dot(place_main[micro], main)
            if plan.rem:
                rest = crecv[micro, :, :, pl.ds(u * pack + unit, lane)]
                rest = dot(place_rem[micro], rest.reshape(plan.lanes_rem, lane))
                each = top * pair_rows
                out = out + jnp.concatenate(
                    [rest[t * each : (t + 1) * each] for t in range(plan.tiles)], axis=1
                )
            x = xs[micro, :, pl.ds(u * unit, unit)].astype(f32)
            for k in range(top):
                x = x + mixing[k, :, :1] * out[k * pair_rows : (k + 1) * pair_rows]
            xs[micro, :, pl.ds(u * unit, unit)] = x.astype(bf16)

        @pl.when(section < last)
        def _():
            relay_copy(micro, g).start()

        @pl.when(jnp.logical_and(section == last, micro < micros - 1))
        def _():
            for block in range(2):
                final_copy(micro, g, block).start()

        @pl.when(jnp.logical_and(section == last, micro == micros - 1))
        def _():
            final_partner_copy(g).start()
            fin[:, fin_cols(own_half, g)] = xs[
                micro, pl.ds(own_block, rows), cols(group)
            ]

    def step(turn, unused):
        first = 2 * turn
        second = first + 1
        every = range(len(groups))
        dispatch_begin(first)
        for g in every:

            @pl.when(turn > 0)
            def _():
                update(first - 1, g)

            dispatch(first, g)
        statistics(first)
        dispatch_begin(second)
        gather_begin()
        gather(first, 0)
        gather(first, 1)
        dispatch(second, 0)
        gather(first, 2)
        dispatch(second, 1)
        gather(first, 3)
        dispatch(second, 2)
        from_partner(first, 3)
        experts_begin(first)
        dispatch(second, 3)
        experts_finish(first, 0)
        experts_finish(first, 1)
        experts_finish(first, 2)
        experts_finish(first, 3)
        statistics(second)
        gather_begin()
        gather(second, 0)
        gather(second, 1)
        gather(second, 2)
        gather(second, 3)
        from_partner(second, 3)
        mix(first)
        experts_begin(second)
        update(first, 0)
        experts_finish(second, 0)
        update(first, 1)
        experts_finish(second, 1)
        update(first, 2)
        experts_finish(second, 2)
        update(first, 3)
        experts_finish(second, 3)
        mix(second)
        return unused

    lax.fori_loop(0, micros // 2, step, 0)
    for g in range(len(groups)):
        update(micros - 1, g)

    for micro in range(max(0, micros - 2), micros):
        hid_copy(micro).wait_send()
        for g in range(len(groups)):
            for rel in range(1, n_pair):
                disp_copy(micro, g, rel).wait_send()
                comb_copy(micro, g, rel).wait_send()
    for micro in range(micros):
        stat_copy(micro).wait_send()
        for g in range(len(groups)):
            fwd_copy(micro, g).wait_send()

    def final_arrival(source, g):
        remote(
            fin.at[:, fin_cols(source * half, g)], fin.at[:, fin_cols(source * half, g)],
            fin_send.at[0, g, 0], fin_recv.at[source, g], partner,
        ).wait_recv()

    @pl.when(section < last)
    def _():
        for g in range(len(groups)):
            for micro in range(micros):
                relay_copy(micro, g).wait_send()
            for source in range(2):
                final_arrival(source, g)

    @pl.when(section == last)
    def _():
        for g in range(len(groups)):
            for micro in range(micros - 1):
                for block in range(2):
                    final_copy(micro, g, block).wait_send()
            final_partner_copy(g).wait_send()
            final_arrival(1 - core, g)

    out_ref[0] = fin[...]


def on_device(inputs, norm_gain, router_weight, gate_weight, up_weight, down_weight, routing):
    micros, rows, width = inputs.shape
    experts, top, hid = router_weight.shape[2], routing.shape[3], gate_weight.shape[2]
    plan = Plan(
        lax.axis_size("pp"), lax.axis_size("ep"), micros, rows, width, experts, top, hid
    )
    n_pair, count, half = plan.n_pair, len(plan.groups), plan.half
    packed = plan.units * plan.pack
    dma, vmem = pltpu.SemaphoreType.DMA, pltpu.VMEM
    any_spec = pl.BlockSpec(memory_space=pl.ANY)
    vmem_spec = pl.BlockSpec(memory_space=pltpu.VMEM)
    picks = plan.lanes_rem if plan.rem else 16
    return pl.pallas_call(
        functools.partial(kernel, plan),
        out_shape=jax.ShapeDtypeStruct((1, rows, width), bf16),
        in_specs=[any_spec, vmem_spec, vmem_spec, any_spec, any_spec, any_spec, vmem_spec],
        out_specs=vmem_spec,
        scratch_shapes=[
            vmem((2, micros, top, rows), jnp.int32),
            vmem((micros, plan.pair_rows, half), bf16),
            vmem((rows, width), bf16),
            vmem((2, n_pair, plan.main, packed), bf16),
            vmem((micros, n_pair, plan.main, packed), bf16),
            vmem((micros, n_pair, plan.main, packed), bf16),
            vmem((2, n_pair, plan.main, packed), bf16),
            vmem((micros, n_pair, plan.main, packed), bf16),
            vmem((width, hid), bf16),
            vmem((width, hid), bf16),
            vmem((2 * hid, half), bf16),
            vmem((2, plan.work_rows, half), bf16),
            vmem((plan.work_rows, lane), f32),
            vmem((plan.work_rows, hid), f32),
            vmem((plan.work_rows, hid), f32),
            vmem((plan.work_rows, half), f32),
            vmem((2, plan.work_rows, hid), bf16),
            vmem((micros, plan.work_rows, hid), bf16),
            vmem((micros, plan.pair_rows, lane), f32),
            vmem((micros, plan.pair_rows, lane), f32),
            vmem((micros, plan.lanes_main, plan.pair_rows), bf16),
            vmem((micros, picks, plan.tiles * plan.pair_rows), bf16),
            vmem((micros, top * plan.pair_rows, plan.lanes_main), bf16),
            vmem((micros, plan.tiles * top * plan.pair_rows, picks), bf16),
            vmem((micros, plan.pair_rows, lane), jnp.int32),
            vmem((top, plan.pair_rows, lane), f32),
            dma((3,)), dma((micros,)), dma, dma, dma((micros,)), dma((micros,)),
            dma((2, count, n_pair)), dma((micros, count, n_pair)),
            dma((micros, count)), dma((micros, count)), dma((2,)), dma((micros,)),
            dma((2, count, n_pair)), dma((micros, count, n_pair)),
            dma((micros,)), dma((micros,)), dma((micros, count)), dma((micros, count)),
            dma((micros, count, 2)), dma((2, count)),
        ],
        compiler_params=pltpu.CompilerParams(
            collective_id=0, has_side_effects=True, vmem_limit_bytes=60 * 1024 * 1024
        ),
    )(
        inputs, norm_gain, router_weight[0].T, gate_weight, up_weight, down_weight,
        jnp.transpose(routing[0], (0, 2, 1)),
    )


def solution(mesh):
    return jax.shard_map(
        on_device,
        mesh=mesh,
        in_specs=(
            P(None, "ep", None),
            P("pp", None),
            P("pp", None, None),
            P("pp", None, "ep"),
            P("pp", None, "ep"),
            P("pp", None, "ep"),
            P("pp", None, "ep", None),
        ),
        out_specs=P("pp", "ep", None),
        check_vma=False,
    )
```

```python
import functools

import jax
import jax.numpy as jnp
from jax import lax
from jax.experimental import pallas as pl
from jax.experimental.pallas import tpu as pltpu
from jax.sharding import PartitionSpec as P

routed_scale = 2.5
norm_epsilon = 1e-06
lane = 128
tile_rows = 16
f32, bf16 = jnp.float32, jnp.bfloat16


class Plan:
    def __init__(self, n_pp, n_ep, micros, rows, width, experts, top, hid):
        self.n_pp, self.n_ep, self.n_pair = n_pp, n_ep, n_ep // 2
        self.micros, self.rows, self.width = micros, rows, width
        self.experts, self.top, self.hid = experts, top, hid
        self.half = width // 2
        self.pair_rows = 2 * rows
        most = rows * top * 5 // (4 * experts)
        slots = 2 * most
        main = tile_rows * max(1, slots // tile_rows)
        extra = max(0, slots - main)
        if extra > tile_rows // 2:
            main, extra = main + tile_rows, 0
        self.main = main
        self.rem = 0 if extra == 0 else (4 if extra <= 4 else 8)
        self.tiles = tile_rows // self.rem if self.rem else 4
        self.unit = lane * self.tiles
        self.pack = self.unit + (lane if self.rem else 0)
        self.units = self.half // self.unit
        self.main_rows = self.n_pair * self.main
        self.rem_rows = self.n_pair * self.rem
        self.work_rows = self.main_rows + self.rem_rows
        self.lanes_main = experts * self.main
        self.lanes_rem = experts * tile_rows
        count = min(4, self.units)
        cuts = [-(-self.units * g // count) for g in range(count + 1)]
        self.groups = list(zip(cuts[:-1], cuts[1:]))


def kernel(
    plan,
    inputs_hbm, gain_ref, router_ref, gate_hbm, up_hbm, down_hbm, routing_ref,
    out_ref,
    routes, xs, dsend, drecv, dpart, csend, crecv, wg, wu, wd,
    lhs, ssq, acc_g, acc_u, acc_d, hid_own, hid_par, stat_own, stat_par,
    pick_main, pick_rem, place_main, place_rem, targets, mixing,
    weight_sem, init_sem, route_send, route_recv, init_send, init_recv,
    disp_send, disp_recv, fwd_send, fwd_recv, hid_send, hid_recv,
    comb_send, comb_recv, stat_send, stat_recv, relay_send, relay_recv, fin_send, fin_recv, ready, keep_sem,
):
    section = lax.axis_index("pp")
    me = lax.axis_index("ep")
    core, pair = me % 2, me // 2
    last = plan.n_pp - 1
    n_pair, rows, half, unit, pack = plan.n_pair, plan.rows, plan.half, plan.unit, plan.pack
    pair_rows, experts, top = plan.pair_rows, plan.experts, plan.top
    groups = plan.groups
    micros = plan.micros
    own_half = pl.multiple_of(core * half, lane)
    par_half = pl.multiple_of((1 - core) * half, lane)
    own_block = pl.multiple_of(core * rows, rows)
    partner = {"ep": me + 1 - 2 * core}

    def flip(value, mask):
        for b in range((n_pair - 1).bit_length()):
            if mask >> b & 1:
                value = value + (1 << b) - 2 * (1 << b) * ((value // (1 << b)) % 2)
        return value

    def remote(src, dst, send, recv, where):
        return pltpu.make_async_remote_copy(
            src_ref=src, dst_ref=dst, send_sem=send, recv_sem=recv,
            device_id=where, device_id_type=pl.DeviceIdType.MESH,
        )

    def dot(a, b):
        return jnp.dot(a, b, preferred_element_type=f32)

    weight_copies = [
        pltpu.make_async_copy(gate_hbm.at[0], wg, weight_sem.at[0]),
        pltpu.make_async_copy(up_hbm.at[0], wu, weight_sem.at[1]),
        pltpu.make_async_copy(down_hbm.at[0], wd, weight_sem.at[2]),
    ]

    def init_local(micro):
        return pltpu.make_async_copy(
            inputs_hbm.at[micro, :, pl.ds(own_half, half)],
            xs.at[micro, pl.ds(own_block, rows), :], init_sem.at[micro],
        )

    def init_copy(micro):
        return remote(
            inputs_hbm.at[micro, :, pl.ds(par_half, half)],
            xs.at[micro, pl.ds(own_block, rows), :],
            init_send.at[micro], init_recv.at[micro], partner,
        )

    route_copy = remote(routing_ref, routes.at[core], route_send, route_recv, partner)

    def cols(group):
        return pl.ds(group[0] * unit, (group[1] - group[0]) * unit)

    def pack_cols(group):
        return pl.ds(group[0] * pack, (group[1] - group[0]) * pack)

    def disp_copy(micro, g, rel):
        to = flip(pair, rel)
        return remote(
            dsend.at[micro % 2, to, :, pack_cols(groups[g])],
            drecv.at[micro, pair, :, pack_cols(groups[g])],
            disp_send.at[micro % 2, g, rel], disp_recv.at[micro, g, rel],
            {"ep": 2 * to + core},
        )

    def fwd_copy(micro, g):
        return remote(
            drecv.at[micro, :, :, pack_cols(groups[g])],
            dpart.at[micro, :, :, pack_cols(groups[g])],
            fwd_send.at[micro, g], fwd_recv.at[micro, g], partner,
        )

    def hid_copy(micro):
        return remote(
            hid_own.at[micro % 2], hid_par.at[micro], hid_send.at[micro % 2], hid_recv.at[micro],
            partner,
        )

    def comb_copy(micro, g, rel):
        to = flip(pair, rel)
        return remote(
            csend.at[micro % 2, to, :, pack_cols(groups[g])],
            crecv.at[micro, pair, :, pack_cols(groups[g])],
            comb_send.at[micro % 2, g, rel], comb_recv.at[micro, g, rel],
            {"ep": 2 * to + core},
        )

    def stat_copy(micro):
        return remote(
            stat_own.at[micro], stat_par.at[micro], stat_send.at[micro], stat_recv.at[micro], partner
        )

    def relay_copy(micro, g):
        ref = xs.at[micro, :, cols(groups[g])]
        return remote(
            ref, ref, relay_send.at[micro, g], relay_recv.at[micro, g],
            {"pp": (section + 1) % plan.n_pp},
        )

    def fin_cols(half_start, g):
        start = pl.multiple_of(half_start + groups[g][0] * unit, lane)
        return pl.ds(start, (groups[g][1] - groups[g][0]) * unit)

    def final_copy(micro, g, block):
        return remote(
            xs.at[micro, pl.ds(block * rows, rows), cols(groups[g])],
            out_ref.at[0, :, fin_cols(own_half, g)],
            fin_send.at[micro, g, block], fin_recv.at[core, g],
            {"pp": micro, "ep": 2 * pair + block},
        )

    def final_partner_copy(g):
        return remote(
            xs.at[micros - 1, pl.ds(pl.multiple_of((1 - core) * rows, rows), rows), cols(groups[g])],
            out_ref.at[0, :, fin_cols(own_half, g)],
            fin_send.at[micros - 1, g, 0], fin_recv.at[core, g], partner,
        )

    def keep_copy(g):
        return pltpu.make_async_copy(
            xs.at[micros - 1, pl.ds(own_block, rows), cols(groups[g])],
            out_ref.at[0, :, fin_cols(own_half, g)], keep_sem.at[g],
        )

    @pl.when(section == 0)
    def _():
        for micro in range(micros):
            init_local(micro).start()

    barrier = pltpu.get_barrier_semaphore()

    def greet(device):
        pl.semaphore_signal(barrier, inc=1, device_id=device, device_id_type=pl.DeviceIdType.MESH)

    near = [{"ep": 2 * flip(pair, rel) + core} for rel in range(1, n_pair)] + [partner]
    for device in near:
        greet(device)

    @pl.when(section < last)
    def _():
        greet({"pp": last})
        greet({"pp": last, "ep": me + 1 - 2 * core})

    @pl.when(section < last - 1)
    def _():
        greet({"pp": section + 1})

    @pl.when(section == 0)
    def _():
        pl.semaphore_wait(barrier, len(near))

    @pl.when(jnp.logical_and(section > 0, section < last))
    def _():
        pl.semaphore_wait(barrier, len(near) + 1)

    @pl.when(section == last)
    def _():
        pl.semaphore_wait(barrier, len(near) + 2 * last)

    @pl.when(section > 0)
    def _():
        pl.semaphore_signal(
            ready, inc=1, device_id={"pp": section - 1}, device_id_type=pl.DeviceIdType.MESH
        )

    route_copy.start()

    @pl.when(section == 0)
    def _():
        for micro in range(micros):
            init_copy(micro).start()

    for copy in weight_copies:
        copy.start()

    routes[core] = routing_ref[...]
    route_copy.wait()

    def make_selections(micro, unused):
        names = jnp.concatenate([routes[0, micro], routes[1, micro]], axis=1)
        expert = lax.broadcasted_iota(jnp.int32, (experts, pair_rows), 0)
        hit = [expert == names[k : k + 1] for k in range(top)]
        chosen = functools.reduce(jnp.logical_or, hit)
        before = lax.broadcasted_iota(jnp.int32, (pair_rows, pair_rows), 0)
        after = lax.broadcasted_iota(jnp.int32, (pair_rows, pair_rows), 1)
        rank = dot(
            jnp.where(chosen, 1.0, 0.0).astype(bf16),
            jnp.where(before < after, 1.0, 0.0).astype(bf16),
        )
        main_target, rem_target, columns = [], [], []
        lanes = lax.broadcasted_iota(jnp.int32, (pair_rows, lane), 1)
        kept = jnp.zeros((pair_rows, lane), jnp.int32)
        for k in range(top):
            slot = jnp.sum(jnp.where(hit[k], rank, 0.0), axis=0, keepdims=True).astype(jnp.int32)
            name = names[k : k + 1]
            main_target.append(jnp.where(slot < plan.main, name * plan.main + slot, -1))
            rem_target.append(
                jnp.where(slot >= plan.main, name * tile_rows + slot - plan.main, -tile_rows * experts)
            )

            def column(row):
                return jnp.sum(
                    jnp.where(before == after, row, 0).astype(f32), axis=1, keepdims=True
                ).astype(jnp.int32)

            columns.append((column(main_target[k]), column(rem_target[k])))
            kept = jnp.where(lanes == k, column(name), kept)
        targets[micro] = kept
        spot = lax.broadcasted_iota(jnp.int32, (plan.lanes_main, pair_rows), 0)
        picks = functools.reduce(jnp.logical_or, [spot == target for target in main_target])
        pick_main[micro] = jnp.where(picks, 1.0, 0.0).astype(bf16)
        spot = lax.broadcasted_iota(jnp.int32, (pair_rows, plan.lanes_main), 1)
        place_main[micro] = jnp.concatenate(
            [jnp.where(spot == columns[k][0], 1.0, 0.0) for k in range(top)], axis=0
        ).astype(bf16)
        if plan.rem:
            spot = lax.broadcasted_iota(jnp.int32, (plan.lanes_rem, pair_rows), 0)
            pick_rem[micro] = jnp.concatenate(
                [
                    jnp.where(
                        functools.reduce(
                            jnp.logical_or, [spot == target + t * plan.rem for target in rem_target]
                        ),
                        1.0, 0.0,
                    )
                    for t in range(plan.tiles)
                ],
                axis=1,
            ).astype(bf16)
            spot = lax.broadcasted_iota(jnp.int32, (pair_rows, plan.lanes_rem), 1)
            place_rem[micro] = jnp.concatenate(
                [
                    jnp.where(spot == columns[k][1] + t * plan.rem, 1.0, 0.0)
                    for t in range(plan.tiles)
                    for k in range(top)
                ],
                axis=0,
            ).astype(bf16)
        return unused

    lax.fori_loop(0, micros, make_selections, 0)

    if plan.rem:
        size = n_pair * tile_rows
        row = lax.broadcasted_iota(jnp.int32, (size, size), 0)
        column = lax.broadcasted_iota(jnp.int32, (size, size), 1)
        rem, tiles = plan.rem, plan.tiles

        def by_tile(index):
            tile, rest = index // (n_pair * rem), index % (n_pair * rem)
            return (rest // rem) * tile_rows + tile * rem + rest % rem

        to_rows = jnp.where(by_tile(row) == column, 1.0, 0.0).astype(bf16)
        to_tiles = jnp.where(by_tile(column) == row, 1.0, 0.0).astype(bf16)

    def dispatch_begin(micro):
        @pl.when(micro >= 2)
        def _():
            for g in range(len(groups)):
                for rel in range(1, n_pair):
                    disp_copy(micro, g, rel).wait_send()

        @pl.when(section == 0)
        def _():
            init_local(micro).wait()
            init_copy(micro).wait()

    def dispatch(micro, g):
        group, pick = groups[g], pick_main[micro]

        @pl.when(section > 0)
        def _():
            relay_copy(micro, g).wait_recv()

        for u in range(*group):
            x = xs[micro, :, pl.ds(u * unit, unit)]
            packed = dot(pick, x).astype(bf16)
            dsend[micro % 2, :, :, pl.ds(u * pack, unit)] = packed.reshape(
                experts, plan.main, unit
            )
            if plan.rem:
                stacked = jnp.concatenate(
                    [x[:, t * lane : (t + 1) * lane] for t in range(plan.tiles)], axis=0
                )
                packed = dot(pick_rem[micro], stacked).astype(bf16)
                dsend[micro % 2, :, :, pl.ds(u * pack + unit, lane)] = packed.reshape(
                    experts, tile_rows, lane
                )
        for rel in reversed(range(1, n_pair)):
            disp_copy(micro, g, rel).start()
        drecv[micro, pair, :, pack_cols(group)] = dsend[micro % 2, pair, :, pack_cols(group)]

    def statistics(micro):
        x = xs[micro].astype(f32)
        lanes = lax.broadcasted_iota(jnp.int32, (pair_rows, lane), 1)
        stat = jnp.where(lanes == experts, jnp.sum(x * x, axis=1, keepdims=True), 0.0)
        scaled = x * gain_ref[:, pl.ds(own_half, half)]
        for e in range(experts):
            weights = router_ref[e : e + 1, pl.ds(own_half, half)].astype(f32)
            stat = jnp.where(lanes == e, jnp.sum(scaled * weights, axis=1, keepdims=True), stat)
        stat_own[micro] = stat
        stat_copy(micro).start()

    def prepare(side, source, micro, group, start):
        for u in range(*group):
            at = pl.ds(u * unit, unit)
            x = source[micro, :, :, pl.ds(u * pack, unit)].reshape(plan.main_rows, unit).astype(f32)
            if plan.rem:
                rest = source[micro, :, :, pl.ds(u * pack + unit, lane)]
                rest = dot(to_rows, rest.reshape(n_pair * tile_rows, lane))
                rest = [
                    rest[t * plan.rem_rows : (t + 1) * plan.rem_rows] for t in range(plan.tiles)
                ]
                x = jnp.concatenate([x, jnp.concatenate(rest, axis=1)], axis=0)
            square = x * x
            ssq[...] += functools.reduce(
                lambda a, b: a + b,
                [square[:, t * lane : (t + 1) * lane] for t in range(plan.tiles)],
            )
            gain = gain_ref[:, pl.ds(pl.multiple_of(start + u * unit, lane), unit)]
            lhs[side, :, at] = (x * gain).astype(bf16)

    def project(side, group, start):
        size = (group[1] - group[0]) * unit
        block = lhs[side, :, cols(group)]
        where = pl.ds(pl.multiple_of(start + group[0] * unit, lane), size)
        acc_g[...] += dot(block, wg[where, :])
        acc_u[...] += dot(block, wu[where, :])

    def gather_begin():
        ssq[...] = jnp.zeros_like(ssq)
        acc_g[...] = jnp.zeros_like(acc_g)
        acc_u[...] = jnp.zeros_like(acc_u)

    def from_partner(micro, g):
        fwd_copy(micro, g).wait_recv()
        prepare(1, dpart, micro, groups[g], par_half)
        project(1, groups[g], par_half)

    def gather(micro, g):
        for rel in range(1, n_pair):
            disp_copy(micro, g, rel).wait_recv()
        fwd_copy(micro, g).start()
        prepare(0, drecv, micro, groups[g], own_half)

        if g == 0:

            @pl.when(micro == 0)
            def _():
                weight_copies[0].wait()
                weight_copies[1].wait()

        project(0, groups[g], own_half)
        if g > 0:
            from_partner(micro, g - 1)

    own_rows = pl.ds(pl.multiple_of(core * plan.hid, plan.hid), plan.hid)
    par_rows = pl.ds(pl.multiple_of((1 - core) * plan.hid, plan.hid), plan.hid)

    def experts_begin(micro):
        @pl.when(micro >= 2)
        def _():
            hid_copy(micro).wait_send()
            for g in range(len(groups)):
                for rel in range(1, n_pair):
                    comb_copy(micro, g, rel).wait_send()

        mean_square = jnp.sum(ssq[...], axis=1, keepdims=True) / plan.width
        scale = lax.rsqrt(mean_square + norm_epsilon)
        gate = acc_g[...] * scale
        hid_own[micro % 2] = (gate / (1.0 + jnp.exp(-gate)) * (acc_u[...] * scale)).astype(bf16)
        hid_copy(micro).start()

    def experts_own(micro):
        @pl.when(micro == 0)
        def _():
            weight_copies[2].wait()

        mine = hid_own[micro % 2]
        for group in groups:
            acc_d[:, cols(group)] = dot(mine, wd[own_rows, cols(group)])

    def experts_finish(micro, g):
        group = groups[g]
        if g == 0:
            hid_copy(micro).wait_recv()
        value = acc_d[:, cols(group)] + dot(hid_par[micro], wd[par_rows, cols(group)])
        value = value.astype(bf16)
        for u in range(*group):
            at = (u - group[0]) * unit
            csend[micro % 2, :, :, pl.ds(u * pack, unit)] = value[
                : plan.main_rows, at : at + unit
            ].reshape(n_pair, plan.main, unit)
            if plan.rem:
                stacked = jnp.concatenate(
                    [
                        value[plan.main_rows :, at + t * lane : at + (t + 1) * lane]
                        for t in range(plan.tiles)
                    ],
                    axis=0,
                )
                csend[micro % 2, :, :, pl.ds(u * pack + unit, lane)] = (
                    dot(to_tiles, stacked).astype(bf16).reshape(n_pair, tile_rows, lane)
                )
        for rel in reversed(range(1, n_pair)):
            comb_copy(micro, g, rel).start()
        crecv[micro, pair, :, pack_cols(group)] = csend[micro % 2, pair, :, pack_cols(group)]

    def mix(micro):
        stat_copy(micro).wait_recv()
        stat = stat_own[micro] + stat_par[micro]
        scale = lax.rsqrt(stat[:, experts : experts + 1] / plan.width + norm_epsilon)
        score = jax.nn.sigmoid(stat * scale)
        lanes = lax.broadcasted_iota(jnp.int32, (pair_rows, lane), 1)
        names = targets[micro]
        picked = [
            jnp.sum(jnp.where(lanes == names[:, k : k + 1], score, 0.0), axis=1, keepdims=True)
            for k in range(top)
        ]
        total = functools.reduce(lambda a, b: a + b, picked)
        for k in range(top):
            mixing[k] = jnp.broadcast_to(routed_scale * picked[k] / total, (pair_rows, lane))

    def update(micro, g):
        group = groups[g]
        for rel in range(1, n_pair):
            comb_copy(micro, g, rel).wait_recv()
        for u in range(*group):
            main = crecv[micro, :, :, pl.ds(u * pack, unit)].reshape(plan.lanes_main, unit)
            out = dot(place_main[micro], main)
            if plan.rem:
                rest = crecv[micro, :, :, pl.ds(u * pack + unit, lane)]
                rest = dot(place_rem[micro], rest.reshape(plan.lanes_rem, lane))
                each = top * pair_rows
                out = out + jnp.concatenate(
                    [rest[t * each : (t + 1) * each] for t in range(plan.tiles)], axis=1
                )
            x = xs[micro, :, pl.ds(u * unit, unit)].astype(f32)
            for k in range(top):
                x = x + mixing[k, :, :1] * out[k * pair_rows : (k + 1) * pair_rows]
            xs[micro, :, pl.ds(u * unit, unit)] = x.astype(bf16)

        if g == 0:

            @pl.when(jnp.logical_and(section < last, micro == 0))
            def _():
                pl.semaphore_wait(ready, 1)

        @pl.when(section < last)
        def _():
            relay_copy(micro, g).start()

        @pl.when(jnp.logical_and(section == last, micro < micros - 1))
        def _():
            for block in range(2):
                final_copy(micro, g, block).start()

        @pl.when(jnp.logical_and(section == last, micro == micros - 1))
        def _():
            final_partner_copy(g).start()
            keep_copy(g).start()

    def step(turn, unused):
        first = 2 * turn
        second = first + 1
        every = range(len(groups))
        dispatch_begin(first)
        for g in every:

            @pl.when(turn > 0)
            def _():
                update(first - 1, g)

            dispatch(first, g)
        statistics(first)
        dispatch_begin(second)
        gather_begin()
        gather(first, 0)
        gather(first, 1)
        dispatch(second, 0)
        gather(first, 2)
        dispatch(second, 1)
        gather(first, 3)
        dispatch(second, 2)
        from_partner(first, 3)
        experts_begin(first)
        experts_own(first)
        dispatch(second, 3)
        experts_finish(first, 0)
        experts_finish(first, 1)
        experts_finish(first, 2)
        experts_finish(first, 3)
        statistics(second)
        gather_begin()
        gather(second, 0)
        gather(second, 1)
        gather(second, 2)
        gather(second, 3)
        from_partner(second, 3)
        mix(first)
        experts_begin(second)
        update(first, 0)
        experts_own(second)
        experts_finish(second, 0)
        update(first, 1)
        experts_finish(second, 1)
        update(first, 2)
        experts_finish(second, 2)
        update(first, 3)
        experts_finish(second, 3)
        mix(second)
        return unused

    lax.fori_loop(0, micros // 2, step, 0)
    for g in range(len(groups)):
        update(micros - 1, g)

    for micro in range(max(0, micros - 2), micros):
        hid_copy(micro).wait_send()
        for g in range(len(groups)):
            for rel in range(1, n_pair):
                disp_copy(micro, g, rel).wait_send()
                comb_copy(micro, g, rel).wait_send()
    for micro in range(micros):
        stat_copy(micro).wait_send()
        for g in range(len(groups)):
            fwd_copy(micro, g).wait_send()

    def final_arrival(source, g):
        remote(
            out_ref.at[0, :, fin_cols(source * half, g)], out_ref.at[0, :, fin_cols(source * half, g)],
            fin_send.at[0, g, 0], fin_recv.at[source, g], partner,
        ).wait_recv()

    @pl.when(section < last)
    def _():
        for g in range(len(groups)):
            for micro in range(micros):
                relay_copy(micro, g).wait_send()
            for source in range(2):
                final_arrival(source, g)

    @pl.when(section == last)
    def _():
        for g in range(len(groups)):
            for micro in range(micros - 1):
                for block in range(2):
                    final_copy(micro, g, block).wait_send()
            final_partner_copy(g).wait_send()
            final_arrival(1 - core, g)
            keep_copy(g).wait()


def on_device(inputs, norm_gain, router_weight, gate_weight, up_weight, down_weight, routing):
    micros, rows, width = inputs.shape
    experts, top, hid = router_weight.shape[2], routing.shape[3], gate_weight.shape[2]
    plan = Plan(
        lax.axis_size("pp"), lax.axis_size("ep"), micros, rows, width, experts, top, hid
    )
    n_pair, count, half = plan.n_pair, len(plan.groups), plan.half
    packed = plan.units * plan.pack
    dma, vmem = pltpu.SemaphoreType.DMA, pltpu.VMEM
    any_spec = pl.BlockSpec(memory_space=pl.ANY)
    vmem_spec = pl.BlockSpec(memory_space=pltpu.VMEM)
    picks = plan.lanes_rem if plan.rem else 16
    return pl.pallas_call(
        functools.partial(kernel, plan),
        out_shape=jax.ShapeDtypeStruct((1, rows, width), bf16),
        in_specs=[any_spec, vmem_spec, vmem_spec, any_spec, any_spec, any_spec, vmem_spec],
        out_specs=any_spec,
        scratch_shapes=[
            vmem((2, micros, top, rows), jnp.int32),
            vmem((micros, plan.pair_rows, half), bf16),
            vmem((2, n_pair, plan.main, packed), bf16),
            vmem((micros, n_pair, plan.main, packed), bf16),
            vmem((micros, n_pair, plan.main, packed), bf16),
            vmem((2, n_pair, plan.main, packed), bf16),
            vmem((micros, n_pair, plan.main, packed), bf16),
            vmem((width, hid), bf16),
            vmem((width, hid), bf16),
            vmem((2 * hid, half), bf16),
            vmem((2, plan.work_rows, half), bf16),
            vmem((plan.work_rows, lane), f32),
            vmem((plan.work_rows, hid), f32),
            vmem((plan.work_rows, hid), f32),
            vmem((plan.work_rows, half), f32),
            vmem((2, plan.work_rows, hid), bf16),
            vmem((micros, plan.work_rows, hid), bf16),
            vmem((micros, plan.pair_rows, lane), f32),
            vmem((micros, plan.pair_rows, lane), f32),
            vmem((micros, plan.lanes_main, plan.pair_rows), bf16),
            vmem((micros, picks, plan.tiles * plan.pair_rows), bf16),
            vmem((micros, top * plan.pair_rows, plan.lanes_main), bf16),
            vmem((micros, plan.tiles * top * plan.pair_rows, picks), bf16),
            vmem((micros, plan.pair_rows, lane), jnp.int32),
            vmem((top, plan.pair_rows, lane), f32),
            dma((3,)), dma((micros,)), dma, dma, dma((micros,)), dma((micros,)),
            dma((2, count, n_pair)), dma((micros, count, n_pair)),
            dma((micros, count)), dma((micros, count)), dma((2,)), dma((micros,)),
            dma((2, count, n_pair)), dma((micros, count, n_pair)),
            dma((micros,)), dma((micros,)), dma((micros, count)), dma((micros, count)),
            dma((micros, count, 2)), dma((2, count)), pltpu.SemaphoreType.REGULAR, dma((count,)),
        ],
        compiler_params=pltpu.CompilerParams(
            collective_id=0, has_side_effects=True, vmem_limit_bytes=60 * 1024 * 1024
        ),
    )(
        inputs, norm_gain, router_weight[0].T, gate_weight, up_weight, down_weight,
        jnp.transpose(routing[0], (0, 2, 1)),
    )


def solution(mesh):
    return jax.shard_map(
        on_device,
        mesh=mesh,
        in_specs=(
            P(None, "ep", None),
            P("pp", None),
            P("pp", None, None),
            P("pp", None, "ep"),
            P("pp", None, "ep"),
            P("pp", None, "ep"),
            P("pp", None, "ep", None),
        ),
        out_specs=P("pp", "ep", None),
        check_vma=False,
    )
```

```python
import functools

import jax
import jax.numpy as jnp
from jax import lax
from jax.experimental import pallas as pl
from jax.experimental.pallas import tpu as pltpu
from jax.sharding import PartitionSpec as P

routed_scale = 2.5
norm_epsilon = 1e-06
lane = 128
tile_rows = 16
f32, bf16 = jnp.float32, jnp.bfloat16


class Plan:
    def __init__(self, n_pp, n_ep, micros, rows, width, experts, top, hid):
        self.n_pp, self.n_ep, self.n_pair = n_pp, n_ep, n_ep // 2
        self.micros, self.rows, self.width = micros, rows, width
        self.experts, self.top, self.hid = experts, top, hid
        self.half = width // 2
        self.pair_rows = 2 * rows
        most = rows * top * 5 // (4 * experts)
        slots = 2 * most
        main = tile_rows * max(1, slots // tile_rows)
        extra = max(0, slots - main)
        if extra > tile_rows // 2:
            main, extra = main + tile_rows, 0
        self.main = main
        self.rem = 0 if extra == 0 else (4 if extra <= 4 else 8)
        self.tiles = tile_rows // self.rem if self.rem else 4
        self.unit = lane * self.tiles
        self.pack = self.unit + (lane if self.rem else 0)
        self.units = self.half // self.unit
        self.main_rows = self.n_pair * self.main
        self.rem_rows = self.n_pair * self.rem
        self.work_rows = self.main_rows + self.rem_rows
        self.lanes_main = experts * self.main
        self.lanes_rem = experts * tile_rows
        count = min(4, self.units)
        cuts = [self.units * g // count for g in range(count + 1)]
        self.groups = list(zip(cuts[:-1], cuts[1:]))


def kernel(
    plan,
    inputs_hbm, gain_ref, router_ref, gate_hbm, up_hbm, down_hbm, routing_ref,
    out_ref,
    routes, xs, dsend, drecv, dpart, csend, crecv, wg, wu, wd,
    lhs, ssq, acc_g, acc_u, acc_d, hid_own, hid_par, stat_own, stat_par,
    pick_main, pick_rem, place_main, place_rem, targets, mixing,
    weight_sem, init_sem, route_send, route_recv, init_send, init_recv,
    disp_send, disp_recv, fwd_send, fwd_recv, hid_send, hid_recv,
    comb_send, comb_recv, stat_send, stat_recv, relay_send, relay_recv, fin_send, fin_recv, ready, keep_sem,
):
    section = lax.axis_index("pp")
    me = lax.axis_index("ep")
    core, pair = me % 2, me // 2
    last = plan.n_pp - 1
    n_pair, rows, half, unit, pack = plan.n_pair, plan.rows, plan.half, plan.unit, plan.pack
    pair_rows, experts, top = plan.pair_rows, plan.experts, plan.top
    groups = plan.groups
    micros = plan.micros
    own_half = pl.multiple_of(core * half, lane)
    par_half = pl.multiple_of((1 - core) * half, lane)
    own_block = pl.multiple_of(core * rows, rows)
    partner = {"ep": me + 1 - 2 * core}

    def flip(value, mask):
        for b in range((n_pair - 1).bit_length()):
            if mask >> b & 1:
                value = value + (1 << b) - 2 * (1 << b) * ((value // (1 << b)) % 2)
        return value

    def remote(src, dst, send, recv, where):
        return pltpu.make_async_remote_copy(
            src_ref=src, dst_ref=dst, send_sem=send, recv_sem=recv,
            device_id=where, device_id_type=pl.DeviceIdType.MESH,
        )

    def dot(a, b):
        return jnp.dot(a, b, preferred_element_type=f32)

    weight_copies = [
        pltpu.make_async_copy(gate_hbm.at[0], wg, weight_sem.at[0]),
        pltpu.make_async_copy(up_hbm.at[0], wu, weight_sem.at[1]),
        pltpu.make_async_copy(down_hbm.at[0], wd, weight_sem.at[2]),
    ]

    def init_local(micro):
        return pltpu.make_async_copy(
            inputs_hbm.at[micro, :, pl.ds(own_half, half)],
            xs.at[micro, pl.ds(own_block, rows), :], init_sem.at[micro],
        )

    def init_copy(micro):
        return remote(
            inputs_hbm.at[micro, :, pl.ds(par_half, half)],
            xs.at[micro, pl.ds(own_block, rows), :],
            init_send.at[micro], init_recv.at[micro], partner,
        )

    route_copy = remote(routing_ref, routes.at[core], route_send, route_recv, partner)

    def cols(group):
        return pl.ds(group[0] * unit, (group[1] - group[0]) * unit)

    def pack_cols(group):
        return pl.ds(group[0] * pack, (group[1] - group[0]) * pack)

    def disp_copy(micro, g, rel):
        to = flip(pair, rel)
        return remote(
            dsend.at[micro % 2, to, :, pack_cols(groups[g])],
            drecv.at[micro, pair, :, pack_cols(groups[g])],
            disp_send.at[micro % 2, g, rel], disp_recv.at[micro, g, rel],
            {"ep": 2 * to + core},
        )

    def fwd_copy(micro, g):
        return remote(
            drecv.at[micro, :, :, pack_cols(groups[g])],
            dpart.at[micro, :, :, pack_cols(groups[g])],
            fwd_send.at[micro, g], fwd_recv.at[micro, g], partner,
        )

    def hid_copy(micro):
        return remote(
            hid_own.at[micro % 2], hid_par.at[micro], hid_send.at[micro % 2], hid_recv.at[micro],
            partner,
        )

    def comb_copy(micro, g, rel):
        to = flip(pair, rel)
        return remote(
            csend.at[micro % 2, to, :, pack_cols(groups[g])],
            crecv.at[micro, pair, :, pack_cols(groups[g])],
            comb_send.at[micro % 2, g, rel], comb_recv.at[micro, g, rel],
            {"ep": 2 * to + core},
        )

    def stat_copy(micro):
        return remote(
            stat_own.at[micro], stat_par.at[micro], stat_send.at[micro], stat_recv.at[micro], partner
        )

    def relay_copy(micro, g):
        ref = xs.at[micro, :, cols(groups[g])]
        return remote(
            ref, ref, relay_send.at[micro, g], relay_recv.at[micro, g],
            {"pp": (section + 1) % plan.n_pp},
        )

    def fin_cols(half_start, g):
        start = pl.multiple_of(half_start + groups[g][0] * unit, lane)
        return pl.ds(start, (groups[g][1] - groups[g][0]) * unit)

    def final_copy(micro, g, block):
        return remote(
            xs.at[micro, pl.ds(block * rows, rows), cols(groups[g])],
            out_ref.at[0, :, fin_cols(own_half, g)],
            fin_send.at[micro, g, block], fin_recv.at[core, g],
            {"pp": micro, "ep": 2 * pair + block},
        )

    def final_partner_copy(g):
        return remote(
            xs.at[micros - 1, pl.ds(pl.multiple_of((1 - core) * rows, rows), rows), cols(groups[g])],
            out_ref.at[0, :, fin_cols(own_half, g)],
            fin_send.at[micros - 1, g, 0], fin_recv.at[core, g], partner,
        )

    def keep_copy(g):
        return pltpu.make_async_copy(
            xs.at[micros - 1, pl.ds(own_block, rows), cols(groups[g])],
            out_ref.at[0, :, fin_cols(own_half, g)], keep_sem.at[g],
        )

    @pl.when(section == 0)
    def _():
        for micro in range(micros):
            init_local(micro).start()

    barrier = pltpu.get_barrier_semaphore()

    def greet(device):
        pl.semaphore_signal(barrier, inc=1, device_id=device, device_id_type=pl.DeviceIdType.MESH)

    near = [{"ep": 2 * flip(pair, rel) + core} for rel in range(1, n_pair)] + [partner]
    for device in near:
        greet(device)

    @pl.when(section < last)
    def _():
        greet({"pp": last})
        greet({"pp": last, "ep": me + 1 - 2 * core})

    @pl.when(section < last - 1)
    def _():
        greet({"pp": section + 1})

    @pl.when(section == 0)
    def _():
        pl.semaphore_wait(barrier, len(near))

    @pl.when(jnp.logical_and(section > 0, section < last))
    def _():
        pl.semaphore_wait(barrier, len(near) + 1)

    @pl.when(section == last)
    def _():
        pl.semaphore_wait(barrier, len(near) + 2 * last)

    @pl.when(section > 0)
    def _():
        pl.semaphore_signal(
            ready, inc=1, device_id={"pp": section - 1}, device_id_type=pl.DeviceIdType.MESH
        )

    route_copy.start()

    @pl.when(section == 0)
    def _():
        for micro in range(micros):
            init_copy(micro).start()

    for copy in weight_copies:
        copy.start()

    routes[core] = routing_ref[...]
    route_copy.wait()

    def make_selections(micro, unused):
        names = jnp.concatenate([routes[0, micro], routes[1, micro]], axis=1)
        expert = lax.broadcasted_iota(jnp.int32, (experts, pair_rows), 0)
        hit = [expert == names[k : k + 1] for k in range(top)]
        chosen = functools.reduce(jnp.logical_or, hit)
        before = lax.broadcasted_iota(jnp.int32, (pair_rows, pair_rows), 0)
        after = lax.broadcasted_iota(jnp.int32, (pair_rows, pair_rows), 1)
        rank = dot(
            jnp.where(chosen, 1.0, 0.0).astype(bf16),
            jnp.where(before < after, 1.0, 0.0).astype(bf16),
        )
        main_target, rem_target, columns = [], [], []
        lanes = lax.broadcasted_iota(jnp.int32, (pair_rows, lane), 1)
        kept = jnp.zeros((pair_rows, lane), jnp.int32)
        for k in range(top):
            slot = jnp.sum(jnp.where(hit[k], rank, 0.0), axis=0, keepdims=True).astype(jnp.int32)
            name = names[k : k + 1]
            main_target.append(jnp.where(slot < plan.main, name * plan.main + slot, -1))
            rem_target.append(
                jnp.where(slot >= plan.main, name * tile_rows + slot - plan.main, -tile_rows * experts)
            )

            def column(row):
                return jnp.sum(
                    jnp.where(before == after, row, 0).astype(f32), axis=1, keepdims=True
                ).astype(jnp.int32)

            columns.append((column(main_target[k]), column(rem_target[k])))
            kept = jnp.where(lanes == k, column(name), kept)
        targets[micro] = kept
        spot = lax.broadcasted_iota(jnp.int32, (plan.lanes_main, pair_rows), 0)
        picks = functools.reduce(jnp.logical_or, [spot == target for target in main_target])
        pick_main[micro] = jnp.where(picks, 1.0, 0.0).astype(bf16)
        spot = lax.broadcasted_iota(jnp.int32, (pair_rows, plan.lanes_main), 1)
        place_main[micro] = jnp.concatenate(
            [jnp.where(spot == columns[k][0], 1.0, 0.0) for k in range(top)], axis=0
        ).astype(bf16)
        if plan.rem:
            spot = lax.broadcasted_iota(jnp.int32, (plan.lanes_rem, pair_rows), 0)
            pick_rem[micro] = jnp.concatenate(
                [
                    jnp.where(
                        functools.reduce(
                            jnp.logical_or, [spot == target + t * plan.rem for target in rem_target]
                        ),
                        1.0, 0.0,
                    )
                    for t in range(plan.tiles)
                ],
                axis=1,
            ).astype(bf16)
            spot = lax.broadcasted_iota(jnp.int32, (pair_rows, plan.lanes_rem), 1)
            place_rem[micro] = jnp.concatenate(
                [
                    jnp.where(spot == columns[k][1] + t * plan.rem, 1.0, 0.0)
                    for t in range(plan.tiles)
                    for k in range(top)
                ],
                axis=0,
            ).astype(bf16)
        return unused

    lax.fori_loop(0, micros, make_selections, 0)

    if plan.rem:
        size = n_pair * tile_rows
        row = lax.broadcasted_iota(jnp.int32, (size, size), 0)
        column = lax.broadcasted_iota(jnp.int32, (size, size), 1)
        rem, tiles = plan.rem, plan.tiles

        def by_tile(index):
            tile, rest = index // (n_pair * rem), index % (n_pair * rem)
            return (rest // rem) * tile_rows + tile * rem + rest % rem

        to_rows = jnp.where(by_tile(row) == column, 1.0, 0.0).astype(bf16)
        to_tiles = jnp.where(by_tile(column) == row, 1.0, 0.0).astype(bf16)

    def dispatch_begin(micro):
        @pl.when(micro >= 2)
        def _():
            for g in range(len(groups)):
                for rel in range(1, n_pair):
                    disp_copy(micro, g, rel).wait_send()

        @pl.when(section == 0)
        def _():
            init_local(micro).wait()
            init_copy(micro).wait()

    def dispatch(micro, g):
        group, pick = groups[g], pick_main[micro]

        @pl.when(section > 0)
        def _():
            relay_copy(micro, g).wait_recv()

        for u in range(*group):
            x = xs[micro, :, pl.ds(u * unit, unit)]
            packed = dot(pick, x).astype(bf16)
            dsend[micro % 2, :, :, pl.ds(u * pack, unit)] = packed.reshape(
                experts, plan.main, unit
            )
            if plan.rem:
                stacked = jnp.concatenate(
                    [x[:, t * lane : (t + 1) * lane] for t in range(plan.tiles)], axis=0
                )
                packed = dot(pick_rem[micro], stacked).astype(bf16)
                dsend[micro % 2, :, :, pl.ds(u * pack + unit, lane)] = packed.reshape(
                    experts, tile_rows, lane
                )
        for rel in reversed(range(1, n_pair)):
            disp_copy(micro, g, rel).start()
        drecv[micro, pair, :, pack_cols(group)] = dsend[micro % 2, pair, :, pack_cols(group)]

    def statistics(micro):
        x = xs[micro].astype(f32)
        lanes = lax.broadcasted_iota(jnp.int32, (pair_rows, lane), 1)
        stat = jnp.where(lanes == experts, jnp.sum(x * x, axis=1, keepdims=True), 0.0)
        scaled = x * gain_ref[:, pl.ds(own_half, half)]
        for e in range(experts):
            weights = router_ref[e : e + 1, pl.ds(own_half, half)].astype(f32)
            stat = jnp.where(lanes == e, jnp.sum(scaled * weights, axis=1, keepdims=True), stat)
        stat_own[micro] = stat
        stat_copy(micro).start()

    def prepare(side, source, micro, group, start):
        for u in range(*group):
            at = pl.ds(u * unit, unit)
            x = source[micro, :, :, pl.ds(u * pack, unit)].reshape(plan.main_rows, unit).astype(f32)
            if plan.rem:
                rest = source[micro, :, :, pl.ds(u * pack + unit, lane)]
                rest = dot(to_rows, rest.reshape(n_pair * tile_rows, lane))
                rest = [
                    rest[t * plan.rem_rows : (t + 1) * plan.rem_rows] for t in range(plan.tiles)
                ]
                x = jnp.concatenate([x, jnp.concatenate(rest, axis=1)], axis=0)
            square = x * x
            ssq[...] += functools.reduce(
                lambda a, b: a + b,
                [square[:, t * lane : (t + 1) * lane] for t in range(plan.tiles)],
            )
            gain = gain_ref[:, pl.ds(pl.multiple_of(start + u * unit, lane), unit)]
            lhs[side, :, at] = (x * gain).astype(bf16)

    def project(side, group, start):
        size = (group[1] - group[0]) * unit
        block = lhs[side, :, cols(group)]
        where = pl.ds(pl.multiple_of(start + group[0] * unit, lane), size)
        acc_g[...] += dot(block, wg[where, :])
        acc_u[...] += dot(block, wu[where, :])

    def gather_begin():
        ssq[...] = jnp.zeros_like(ssq)
        acc_g[...] = jnp.zeros_like(acc_g)
        acc_u[...] = jnp.zeros_like(acc_u)

    def from_partner(micro, g):
        fwd_copy(micro, g).wait_recv()
        prepare(1, dpart, micro, groups[g], par_half)
        project(1, groups[g], par_half)

    def gather(micro, g):
        for rel in range(1, n_pair):
            disp_copy(micro, g, rel).wait_recv()
        fwd_copy(micro, g).start()
        prepare(0, drecv, micro, groups[g], own_half)

        if g == 0:

            @pl.when(micro == 0)
            def _():
                weight_copies[0].wait()
                weight_copies[1].wait()

        project(0, groups[g], own_half)
        if g > 0:
            from_partner(micro, g - 1)

    own_rows = pl.ds(pl.multiple_of(core * plan.hid, plan.hid), plan.hid)
    par_rows = pl.ds(pl.multiple_of((1 - core) * plan.hid, plan.hid), plan.hid)

    def experts_begin(micro):
        @pl.when(micro >= 2)
        def _():
            hid_copy(micro).wait_send()
            for g in range(len(groups)):
                for rel in range(1, n_pair):
                    comb_copy(micro, g, rel).wait_send()

        mean_square = jnp.sum(ssq[...], axis=1, keepdims=True) / plan.width
        scale = lax.rsqrt(mean_square + norm_epsilon)
        gate = acc_g[...] * scale
        hid_own[micro % 2] = (gate / (1.0 + jnp.exp(-gate)) * (acc_u[...] * scale)).astype(bf16)
        hid_copy(micro).start()

    def experts_own(micro):
        @pl.when(micro == 0)
        def _():
            weight_copies[2].wait()

        mine = hid_own[micro % 2]
        for group in groups:
            acc_d[:, cols(group)] = dot(mine, wd[own_rows, cols(group)])

    def experts_finish(micro, g):
        group = groups[g]
        if g == 0:
            hid_copy(micro).wait_recv()
        value = acc_d[:, cols(group)] + dot(hid_par[micro], wd[par_rows, cols(group)])
        value = value.astype(bf16)
        for u in range(*group):
            at = (u - group[0]) * unit
            csend[micro % 2, :, :, pl.ds(u * pack, unit)] = value[
                : plan.main_rows, at : at + unit
            ].reshape(n_pair, plan.main, unit)
            if plan.rem:
                stacked = jnp.concatenate(
                    [
                        value[plan.main_rows :, at + t * lane : at + (t + 1) * lane]
                        for t in range(plan.tiles)
                    ],
                    axis=0,
                )
                csend[micro % 2, :, :, pl.ds(u * pack + unit, lane)] = (
                    dot(to_tiles, stacked).astype(bf16).reshape(n_pair, tile_rows, lane)
                )
        for rel in reversed(range(1, n_pair)):
            comb_copy(micro, g, rel).start()
        crecv[micro, pair, :, pack_cols(group)] = csend[micro % 2, pair, :, pack_cols(group)]

    def mix(micro):
        stat_copy(micro).wait_recv()
        stat = stat_own[micro] + stat_par[micro]
        scale = lax.rsqrt(stat[:, experts : experts + 1] / plan.width + norm_epsilon)
        score = jax.nn.sigmoid(stat * scale)
        lanes = lax.broadcasted_iota(jnp.int32, (pair_rows, lane), 1)
        names = targets[micro]
        picked = [
            jnp.sum(jnp.where(lanes == names[:, k : k + 1], score, 0.0), axis=1, keepdims=True)
            for k in range(top)
        ]
        total = functools.reduce(lambda a, b: a + b, picked)
        for k in range(top):
            mixing[k] = jnp.broadcast_to(routed_scale * picked[k] / total, (pair_rows, lane))

    def update(micro, g):
        group = groups[g]
        for rel in range(1, n_pair):
            comb_copy(micro, g, rel).wait_recv()
        for u in range(*group):
            main = crecv[micro, :, :, pl.ds(u * pack, unit)].reshape(plan.lanes_main, unit)
            out = dot(place_main[micro], main)
            if plan.rem:
                rest = crecv[micro, :, :, pl.ds(u * pack + unit, lane)]
                rest = dot(place_rem[micro], rest.reshape(plan.lanes_rem, lane))
                each = top * pair_rows
                out = out + jnp.concatenate(
                    [rest[t * each : (t + 1) * each] for t in range(plan.tiles)], axis=1
                )
            x = xs[micro, :, pl.ds(u * unit, unit)].astype(f32)
            for k in range(top):
                x = x + mixing[k, :, :1] * out[k * pair_rows : (k + 1) * pair_rows]
            xs[micro, :, pl.ds(u * unit, unit)] = x.astype(bf16)

        if g == 0:

            @pl.when(jnp.logical_and(section < last, micro == 0))
            def _():
                pl.semaphore_wait(ready, 1)

        @pl.when(section < last)
        def _():
            relay_copy(micro, g).start()

        @pl.when(jnp.logical_and(section == last, micro < micros - 1))
        def _():
            for block in range(2):
                final_copy(micro, g, block).start()

        @pl.when(jnp.logical_and(section == last, micro == micros - 1))
        def _():
            final_partner_copy(g).start()
            keep_copy(g).start()

    def step(turn, unused):
        first = 2 * turn
        second = first + 1
        every = range(len(groups))
        dispatch_begin(first)
        for g in every:

            @pl.when(turn > 0)
            def _():
                update(first - 1, g)

            dispatch(first, g)
        statistics(first)
        dispatch_begin(second)
        gather_begin()
        gather(first, 0)
        gather(first, 1)
        dispatch(second, 0)
        gather(first, 2)
        dispatch(second, 1)
        gather(first, 3)
        dispatch(second, 2)
        from_partner(first, 3)
        experts_begin(first)
        experts_own(first)
        dispatch(second, 3)
        experts_finish(first, 0)
        experts_finish(first, 1)
        experts_finish(first, 2)
        experts_finish(first, 3)
        gather_begin()
        gather(second, 0)
        gather(second, 1)
        gather(second, 2)
        gather(second, 3)
        from_partner(second, 3)
        experts_begin(second)
        mix(first)
        update(first, 0)
        experts_own(second)
        update(first, 1)
        experts_finish(second, 0)
        experts_finish(second, 1)
        statistics(second)
        update(first, 2)
        experts_finish(second, 2)
        update(first, 3)
        experts_finish(second, 3)
        mix(second)
        return unused

    lax.fori_loop(0, micros // 2, step, 0)
    for g in range(len(groups)):
        update(micros - 1, g)

    for micro in range(max(0, micros - 2), micros):
        hid_copy(micro).wait_send()
        for g in range(len(groups)):
            for rel in range(1, n_pair):
                disp_copy(micro, g, rel).wait_send()
                comb_copy(micro, g, rel).wait_send()
    for micro in range(micros):
        stat_copy(micro).wait_send()
        for g in range(len(groups)):
            fwd_copy(micro, g).wait_send()

    def final_arrival(source, g):
        remote(
            out_ref.at[0, :, fin_cols(source * half, g)], out_ref.at[0, :, fin_cols(source * half, g)],
            fin_send.at[0, g, 0], fin_recv.at[source, g], partner,
        ).wait_recv()

    @pl.when(section < last)
    def _():
        for g in range(len(groups)):
            for micro in range(micros):
                relay_copy(micro, g).wait_send()
            for source in range(2):
                final_arrival(source, g)

    @pl.when(section == last)
    def _():
        for g in range(len(groups)):
            for micro in range(micros - 1):
                for block in range(2):
                    final_copy(micro, g, block).wait_send()
            final_partner_copy(g).wait_send()
            final_arrival(1 - core, g)
            keep_copy(g).wait()


def on_device(inputs, norm_gain, router_weight, gate_weight, up_weight, down_weight, routing):
    micros, rows, width = inputs.shape
    experts, top, hid = router_weight.shape[2], routing.shape[3], gate_weight.shape[2]
    plan = Plan(
        lax.axis_size("pp"), lax.axis_size("ep"), micros, rows, width, experts, top, hid
    )
    n_pair, count, half = plan.n_pair, len(plan.groups), plan.half
    packed = plan.units * plan.pack
    dma, vmem = pltpu.SemaphoreType.DMA, pltpu.VMEM
    any_spec = pl.BlockSpec(memory_space=pl.ANY)
    vmem_spec = pl.BlockSpec(memory_space=pltpu.VMEM)
    picks = plan.lanes_rem if plan.rem else 16
    return pl.pallas_call(
        functools.partial(kernel, plan),
        out_shape=jax.ShapeDtypeStruct((1, rows, width), bf16),
        in_specs=[any_spec, vmem_spec, vmem_spec, any_spec, any_spec, any_spec, vmem_spec],
        out_specs=any_spec,
        scratch_shapes=[
            vmem((2, micros, top, rows), jnp.int32),
            vmem((micros, plan.pair_rows, half), bf16),
            vmem((2, n_pair, plan.main, packed), bf16),
            vmem((micros, n_pair, plan.main, packed), bf16),
            vmem((micros, n_pair, plan.main, packed), bf16),
            vmem((2, n_pair, plan.main, packed), bf16),
            vmem((micros, n_pair, plan.main, packed), bf16),
            vmem((width, hid), bf16),
            vmem((width, hid), bf16),
            vmem((2 * hid, half), bf16),
            vmem((2, plan.work_rows, half), bf16),
            vmem((plan.work_rows, lane), f32),
            vmem((plan.work_rows, hid), f32),
            vmem((plan.work_rows, hid), f32),
            vmem((plan.work_rows, half), f32),
            vmem((2, plan.work_rows, hid), bf16),
            vmem((micros, plan.work_rows, hid), bf16),
            vmem((micros, plan.pair_rows, lane), f32),
            vmem((micros, plan.pair_rows, lane), f32),
            vmem((micros, plan.lanes_main, plan.pair_rows), bf16),
            vmem((micros, picks, plan.tiles * plan.pair_rows), bf16),
            vmem((micros, top * plan.pair_rows, plan.lanes_main), bf16),
            vmem((micros, plan.tiles * top * plan.pair_rows, picks), bf16),
            vmem((micros, plan.pair_rows, lane), jnp.int32),
            vmem((top, plan.pair_rows, lane), f32),
            dma((3,)), dma((micros,)), dma, dma, dma((micros,)), dma((micros,)),
            dma((2, count, n_pair)), dma((micros, count, n_pair)),
            dma((micros, count)), dma((micros, count)), dma((2,)), dma((micros,)),
            dma((2, count, n_pair)), dma((micros, count, n_pair)),
            dma((micros,)), dma((micros,)), dma((micros, count)), dma((micros, count)),
            dma((micros, count, 2)), dma((2, count)), pltpu.SemaphoreType.REGULAR, dma((count,)),
        ],
        compiler_params=pltpu.CompilerParams(
            collective_id=0, has_side_effects=True, vmem_limit_bytes=60 * 1024 * 1024
        ),
    )(
        inputs, norm_gain, router_weight[0].T, gate_weight, up_weight, down_weight,
        jnp.transpose(routing[0], (0, 2, 1)),
    )


def solution(mesh):
    return jax.shard_map(
        on_device,
        mesh=mesh,
        in_specs=(
            P(None, "ep", None),
            P("pp", None),
            P("pp", None, None),
            P("pp", None, "ep"),
            P("pp", None, "ep"),
            P("pp", None, "ep"),
            P("pp", None, "ep", None),
        ),
        out_specs=P("pp", "ep", None),
        check_vma=False,
    )
```
